32 devices in a mesh: rep: 4 (over y, x), shard: 8 (over z, core).
Axes of the slice: x: 2, y: 2, z: 4, core: 2. Of those that a mesh axis runs over, the one named last changes fastest.
Arguments:
- tokens: bfloat16 [12288, 1024], P(('rep', 'shard')), may hold values from -6 to 6
- time_features: bfloat16 [12288, 1024], P(('rep', 'shard')), may hold values from -1 to 1
- out_grad: bfloat16 [12288, 1024], P(('rep', 'shard')), may hold values from -6 to 6
- deal: int32 [12288], P('rep'), may hold values from 0 to 3071, as said below
- seq_lengths: int32 [32, 4], P(('rep', 'shard')), may hold values from 1 to 192, as said below
- seq_offsets: int32 [32, 4], P(('rep', 'shard')), may hold values from 0 to 383, as said below
- time_weight: bfloat16 [1024, 1024], P('shard'), may hold values from -0.1875 to 0.1875
- time_bias: bfloat16 [1024], P('shard'), may hold values from -2 to 2
- qkv_weight: bfloat16 [2, 1024, 3072], P(None, 'shard'), may hold values from -0.1875 to 0.1875
- qv_bias: bfloat16 [2, 2048], P(None, 'shard'), may hold values from -2 to 2
- out_weight: bfloat16 [2, 1024, 1024], P(None, 'shard'), may hold values from -1 to 1
- out_bias: bfloat16 [2, 1024], P(None, 'shard'), may hold values from -2 to 2
- norm1_gain: bfloat16 [2, 1024], P(None, 'shard'), may hold values from 0.5 to 1.5
- norm1_bias: bfloat16 [2, 1024], P(None, 'shard'), may hold values from -2 to 2
- ffin_weight: bfloat16 [2, 1024, 4096], P(None, 'shard'), may hold values from -0.1875 to 0.1875
- ffin_bias: bfloat16 [2, 4096], P(None, 'shard'), may hold values from -2 to 2
- ffout_weight: bfloat16 [2, 4096, 1024], P(None, 'shard'), may hold values from -0.09375 to 0.09375
- ffout_bias: bfloat16 [2, 1024], P(None, 'shard'), may hold values from -2 to 2
- norm2_gain: bfloat16 [2, 1024], P(None, 'shard'), may hold values from 0.5 to 1.5
- norm2_bias: bfloat16 [2, 1024], P(None, 'shard'), may hold values from -2 to 2
Outputs:
- hidden: bfloat16 [12288, 1024], P(('rep', 'shard'))
- input_grad: bfloat16 [12288, 1024], P(('rep', 'shard'))
- time_weight_grad: float32 [1024, 1024], P('shard')
- time_bias_grad: float32 [1024], P('shard')
- qkv_weight_grad: float32 [2, 1024, 3072], P(None, 'shard')
- qv_bias_grad: float32 [2, 2048], P(None, 'shard')
- out_weight_grad: float32 [2, 1024, 1024], P(None, 'shard')
- out_bias_grad: float32 [2, 1024], P(None, 'shard')
- norm1_gain_grad: float32 [2, 1024], P(None, 'shard')
- norm1_bias_grad: float32 [2, 1024], P(None, 'shard')
- ffin_weight_grad: float32 [2, 1024, 4096], P(None, 'shard')
- ffin_bias_grad: float32 [2, 4096], P(None, 'shard')
- ffout_weight_grad: float32 [2, 4096, 1024], P(None, 'shard')
- ffout_bias_grad: float32 [2, 1024], P(None, 'shard')
- norm2_gain_grad: float32 [2, 1024], P(None, 'shard')
- norm2_bias_grad: float32 [2, 1024], P(None, 'shard')
The draws below stay inside these ranges and needn't reach their ends.
Inputs may be any that keep to these rules, and one draw needn't show every extreme that they name: `deal`: each block of 3072 entries (one replica group) is a permutation of 0 to 3071; every aligned run of 384 entries in it names exactly 48 rows of each device's dealt layout. `seq_lengths`: each row holds the lengths of one device's 4 dealt sequences; they sum to 384 and one of them is exactly 192. `seq_offsets`: each row holds the first rows of those sequences: 0, then each the sum of the lengths before it.
All inputs are finite; a program needn't handle non-finite values.
Results may differ from the reference program's by a relative error of at most 0.028.
Values may be sent and summed in bfloat16 or wider, within the bound.
No kernel may reach another device: no remote copies, remote signals or barrier semaphores. Data moves between devices by JAX's collectives and lax.ppermute only.
A program may use at most 256 MiB of HBM per device.

```python
import math
import jax
import jax.numpy as jnp
from jax import lax

D = 1024
HEADS = 16
HEAD_DIM = 64
FF = 4096
LAYERS = 2
TOK_DEV = 384
SEQ_DEV = 4
MOST = 192
TOKENS = 12288
N_REP = 4
N_SHARD = 8


def lengths_common(key):
    row_count = N_REP * N_SHARD
    remain = TOK_DEV - MOST
    first_key = jax.random.fold_in(key, 11)
    second_key = jax.random.fold_in(key, 12)
    order_key = jax.random.fold_in(key, 13)
    first_cut = jax.random.randint(first_key, (row_count,), 1, remain - 1)
    second_cut = jax.random.randint(second_key, (row_count,), first_cut + 1, remain)
    pieces = jnp.stack([jnp.full((row_count,), MOST, jnp.int32), first_cut, second_cut - first_cut, remain - second_cut], axis=1).astype(jnp.int32)
    row_keys = jax.random.split(order_key, row_count)
    orders = jax.vmap(lambda row_key: jax.random.permutation(row_key, SEQ_DEV))(row_keys)
    return jnp.take_along_axis(pieces, orders.astype(jnp.int32), axis=1).astype(jnp.int32)


def draw_seq_lengths(key, part):
    return lengths_common(key)


def draw_seq_offsets(key, part):
    lengths = lengths_common(key)
    return (jnp.cumsum(lengths, axis=1) - lengths).astype(jnp.int32)


def draw_deal(key, part):
    pair_rows = TOK_DEV // N_SHARD
    dest_key = jax.random.fold_in(key, 21)
    source_key = jax.random.fold_in(key, 22)
    dest_keys = jax.random.split(dest_key, N_REP * N_SHARD)
    shuffled = jax.vmap(lambda one_key: jax.random.permutation(one_key, TOK_DEV))(dest_keys)
    shuffled = shuffled.astype(jnp.int32).reshape(N_REP, N_SHARD, N_SHARD, pair_rows)
    dest_index = jnp.arange(N_SHARD, dtype=jnp.int32)[None, :, None, None]
    values = dest_index * TOK_DEV + shuffled
    values = jnp.transpose(values, (0, 2, 1, 3)).reshape(N_REP * N_SHARD, TOK_DEV)
    source_keys = jax.random.split(source_key, N_REP * N_SHARD)
    mixing = jax.vmap(lambda one_key: jax.random.permutation(one_key, TOK_DEV))(source_keys).astype(jnp.int32)
    values = jnp.take_along_axis(values, mixing, axis=1)
    return values.reshape(N_REP * N_SHARD * TOK_DEV).astype(jnp.int32)


def level_of(key, shape, cuts, smallest, top_value):
    loudness, own = 1.0, jax.random.fold_in(key, 6)
    for dim, parts in cuts:
        draws = jnp.exp(jax.random.uniform(jax.random.fold_in(own, dim), (parts,), jnp.float32, smallest / len(cuts), top_value / len(cuts)))
        loudness = loudness * jnp.repeat(draws, shape[dim] // parts).reshape([-1 if axis == dim else 1 for axis in range(len(shape))])
    return loudness


def gaussian(own_key, dims, scale, bound, shards=(), kind=jnp.bfloat16):
    array = scale * jax.random.normal(own_key, dims, jnp.float32)
    if shards:
        array = array * level_of(own_key, dims, shards, -0.22, 0.18)
    return jnp.clip(array, -bound, bound).astype(kind)


def setup_inputs(seed: int = 0) -> dict:
    key_of = jax.random.split(jax.random.key(seed), 21)
    tokens = gaussian(key_of[0], (TOKENS, D), 1.0, 6.0, ((0, 32),))
    time_features = jnp.clip(jax.random.uniform(key_of[1], (TOKENS, D), jnp.float32, -1.0, 1.0) * level_of(key_of[1], (TOKENS, D), ((0, 32),), -0.4, 0.0), -1.0, 1.0).astype(jnp.bfloat16)
    out_grad = gaussian(key_of[2], (TOKENS, D), 1.0, 6.0, ((0, 32),))
    deal = draw_deal(jax.random.fold_in(key_of[20], 71), 0)
    seq_lengths = draw_seq_lengths(jax.random.fold_in(key_of[20], 71), 0)
    seq_offsets = draw_seq_offsets(jax.random.fold_in(key_of[20], 71), 0)
    time_weight = gaussian(key_of[6], (D, D), D ** -0.5, 0.1875, ((0, 8),))
    time_bias = gaussian(key_of[7], (D,), 0.3, 2.0, ((0, 8),))
    qkv_weight = gaussian(key_of[8], (LAYERS, D, 3 * D), D ** -0.5, 0.1875, ((1, 8),))
    qv_bias = gaussian(key_of[9], (LAYERS, 2 * D), 0.3, 2.0, ((1, 8),))
    out_weight = gaussian(key_of[10], (LAYERS, D, D), (D // 32) ** -0.5, 1.0, ((1, 8),))
    out_bias = gaussian(key_of[11], (LAYERS, D), 0.3, 2.0, ((1, 8),))
    norm1_gain = jnp.clip(1.0 + 0.1 * jax.random.normal(key_of[12], (LAYERS, D), jnp.float32), 0.5, 1.5).astype(jnp.bfloat16)
    norm1_bias = gaussian(key_of[13], (LAYERS, D), 0.3, 2.0, ((1, 8),))
    ffin_weight = gaussian(key_of[14], (LAYERS, D, FF), D ** -0.5, 0.1875, ((1, 8),))
    ffin_bias = gaussian(key_of[15], (LAYERS, FF), 0.3, 2.0, ((1, 8),))
    ffout_weight = gaussian(key_of[16], (LAYERS, FF, D), FF ** -0.5, 0.09375, ((1, 8),))
    ffout_bias = gaussian(key_of[17], (LAYERS, D), 0.3, 2.0, ((1, 8),))
    norm2_gain = jnp.clip(1.0 + 0.1 * jax.random.normal(key_of[18], (LAYERS, D), jnp.float32), 0.5, 1.5).astype(jnp.bfloat16)
    norm2_bias = gaussian(key_of[19], (LAYERS, D), 0.3, 2.0, ((1, 8),))
    return dict(tokens=tokens, time_features=time_features, out_grad=out_grad, deal=deal, seq_lengths=seq_lengths, seq_offsets=seq_offsets, time_weight=time_weight, time_bias=time_bias, qkv_weight=qkv_weight, qv_bias=qv_bias, out_weight=out_weight, out_bias=out_bias, norm1_gain=norm1_gain, norm1_bias=norm1_bias, ffin_weight=ffin_weight, ffin_bias=ffin_bias, ffout_weight=ffout_weight, ffout_bias=ffout_bias, norm2_gain=norm2_gain, norm2_bias=norm2_bias)


@jax.custom_vjp
def low(v):
    return lax.optimization_barrier(v.astype(jnp.bfloat16)).astype(jnp.float32)

@jax.custom_vjp
def low_back(v):
    return v

def low_keep(v):
    return (low(v), None)

def low_pass(kept, grad):
    return (grad,)

def back_keep(v):
    return (v, None)

def back_low(kept, grad):
    return (low(grad),)
low.defvjp(low_keep, low_pass)
low_back.defvjp(back_keep, back_low)
highest = lax.Precision.HIGHEST
epsilon = 1e-05
negative = -1e+30

def matmul_rows(left, right):
    return jnp.einsum('...d,de->...e', left, right, precision=highest)

def layer_norm(values, gain, shift):
    centred = values - lax.optimization_barrier(jnp.mean(values, axis=-1, keepdims=True))
    spread = lax.optimization_barrier(jnp.mean(centred * centred, axis=-1, keepdims=True))
    return centred * lax.rsqrt(spread + epsilon) * gain + shift

def attend(packed):
    qkv_rows, visible = packed
    rows = qkv_rows.shape[0]
    queries = qkv_rows[:, :D].reshape(rows, HEADS, HEAD_DIM)
    key_rows = qkv_rows[:, D:2 * D].reshape(rows, HEADS, HEAD_DIM)
    value_rows = qkv_rows[:, 2 * D:].reshape(rows, HEADS, HEAD_DIM)
    scale = 1.0 / math.sqrt(HEAD_DIM)
    scores = low_back(jnp.einsum('qhd,khd->hqk', queries, key_rows, precision=highest) * scale)
    scores = jnp.where(visible[None], scores, negative)
    peak = lax.optimization_barrier(jnp.max(scores, axis=-1, keepdims=True))
    expo = jnp.exp(scores - peak)
    probs = low(expo / lax.optimization_barrier(jnp.sum(expo, axis=-1, keepdims=True)))
    mixed = jnp.einsum('hqk,khd->qhd', probs, value_rows, precision=highest)
    return mixed.reshape(rows, D)

def encoder_block(hidden, params, visible):
    qkv_w, qv_b, out_w, out_b, gain_one, shift_one, ffin_w, ffin_b, ffout_w, ffout_b, gain_two, shift_two = params
    hidden_b = low(hidden)
    bias_full = jnp.concatenate([qv_b[:D], jnp.zeros((D,), jnp.float32), qv_b[D:]])
    qkv = low(low_back(matmul_rows(hidden_b, qkv_w) + bias_full))
    mixed = lax.map(jax.checkpoint(attend), (qkv, visible))
    mixed = low(low_back(mixed))
    first = layer_norm(hidden + low_back(matmul_rows(mixed, out_w) + out_b), gain_one, shift_one)
    first_b = low(first)
    inner = low_back(matmul_rows(first_b, ffin_w) + ffin_b)
    active = low(jax.nn.gelu(inner, approximate=False))
    return layer_norm(first + low_back(matmul_rows(active, ffout_w) + ffout_b), gain_two, shift_two)

def widen(values):
    return values.astype(jnp.float32)

def reference(tokens, time_features, out_grad, deal, seq_lengths, seq_offsets, time_weight, time_bias, qkv_weight, qv_bias, out_weight, out_bias, norm1_gain, norm1_bias, ffin_weight, ffin_bias, ffout_weight, ffout_bias, norm2_gain, norm2_bias):
    rows_total = tokens.shape[0]
    group_rows = N_SHARD * TOK_DEV
    buffers = N_REP * N_SHARD
    base = jnp.arange(rows_total, dtype=jnp.int32) // group_rows * group_rows
    place = (base + deal).astype(jnp.int32)
    source_of = jnp.zeros((rows_total,), jnp.int32).at[place].set(jnp.arange(rows_total, dtype=jnp.int32))
    positions = jnp.arange(TOK_DEV, dtype=jnp.int32)
    starts = seq_offsets[:, :, None]
    finish = starts + seq_lengths[:, :, None]
    member = (positions[None, None, :] >= starts) & (positions[None, None, :] < finish)
    visible = jnp.any(member[:, :, :, None] & member[:, :, None, :], axis=1)
    visible = visible | (positions[:, None] == positions[None, :])[None]
    feature_f = widen(time_features)
    layer_params = (widen(qkv_weight), widen(qv_bias), widen(out_weight), widen(out_bias), widen(norm1_gain), widen(norm1_bias), widen(ffin_weight), widen(ffin_bias), widen(ffout_weight), widen(ffout_bias), widen(norm2_gain), widen(norm2_bias))

    def forward(token_f, time_w, time_b, params):
        embed = low_back(matmul_rows(feature_f, time_w) + time_b)
        hidden = token_f + embed
        hidden = hidden[source_of].reshape(buffers, TOK_DEV, D)
        for layer_at in range(LAYERS):
            hidden = encoder_block(hidden, tuple((piece[layer_at] for piece in params)), visible)
        return hidden.reshape(rows_total, D)[place]
    outputs, pullback = jax.vjp(forward, widen(tokens), widen(time_weight), widen(time_bias), layer_params)
    token_grad, time_w_grad, time_b_grad, layer_grads = pullback(widen(out_grad))
    return (outputs.astype(jnp.bfloat16), token_grad.astype(jnp.bfloat16), time_w_grad, time_b_grad, layer_grads[0], layer_grads[1], layer_grads[2], layer_grads[3], layer_grads[4], layer_grads[5], layer_grads[6], layer_grads[7], layer_grads[8], layer_grads[9], layer_grads[10], layer_grads[11])
```

```python
import functools
import math

import jax
import jax.numpy as jnp
from jax import lax
from jax.experimental import pallas as pl
from jax.experimental.pallas import tpu as pltpu
from jax.sharding import PartitionSpec as P

HEADS = 16
LAYERS = 2
SMALL_ROWS = 16


epsilon = 1e-05
negative = -1e30

def layer_norm(values, gain, shift):
    centred = values - jnp.mean(values, axis=-1, keepdims=True)
    spread = jnp.mean(centred * centred, axis=-1, keepdims=True)
    return centred * lax.rsqrt(spread + epsilon) * gain + shift


def product(left, right):
    return jnp.dot(left, right, preferred_element_type=jnp.float32)


def contract_rows(left, right):
    return lax.dot_general(
        left, right, (((0,), (0,)), ((), ())), preferred_element_type=jnp.float32
    )


def times_transposed(left, right):
    return lax.dot_general(
        left, right, (((1,), (1,)), ((), ())), preferred_element_type=jnp.float32
    )


def column_sums(values):
    return jnp.sum(values.astype(jnp.float32), axis=0)


def split_heads(block_rows, heads):
    return block_rows.reshape(block_rows.shape[0], heads, -1)


def head_blocks(qkv_rows, width, heads):
    queries = split_heads(qkv_rows[:, :width], heads)
    key_rows = split_heads(qkv_rows[:, width : 2 * width], heads)
    value_rows = split_heads(qkv_rows[:, 2 * width :], heads)
    return (queries, key_rows, value_rows)


def masked_scores(queries, key_rows, visible, scale):
    scores = (
        jnp.einsum("qhd,khd->hqk", queries, key_rows, preferred_element_type=jnp.float32) * scale
    )
    return jnp.where(visible[None], scores, negative)


def bits_of(count):
    return [1 << k for k in range(count.bit_length() - 1)]


def swap_rep(value, bit, n_rep):
    return lax.ppermute(value, "rep", [(i, i ^ bit) for i in range(n_rep)])


def swap_shard(value, bit, n_shard):
    return lax.ppermute(value, "shard", [(i, i ^ bit) for i in range(n_shard)])


def gather_z(piece, n_shard):
    z_bits = bits_of(n_shard)[1:][::-1]
    have, offsets = [piece[None]], [0]
    for at, bit in enumerate(z_bits):
        send = have[0] if at == 0 else jnp.concatenate(have)
        have.append(swap_shard(send, bit, n_shard))
        offsets = offsets + [o ^ (bit >> 1) for o in offsets]
    return jnp.concatenate(have[1:]), offsets[1:]


def gather_rep(pieces, n_rep, order):
    have, offsets = [pieces[None]], [0]
    send = have[0]
    for at, bit in enumerate(order):
        send = have[0] if at == 0 else jnp.concatenate(have)
        have.append(swap_rep(send, bit, n_rep))
        offsets = offsets + [o ^ bit for o in offsets]
    return send, have[-1], offsets


def assemble_kernel(me_ref, local_ref, other_ref, *refs, spec):
    low, high, clow, chigh, out_ref, buf, in_sem, out_sem = refs
    layer, rows, cols, n, off, row_blocks, z_off, r_off, o_off = spec
    rep, shard = me_ref[0], me_ref[1]
    local = local_ref if layer is None else local_ref.at[layer]
    height = rows * row_blocks
    half = len(r_off) // 2
    per = cols // n

    def start(src, dst, at):
        pltpu.make_async_copy(src, dst, in_sem.at[at]).start()

    start(local, buf.at[pl.ds(shard * height, height), :], 0)
    base = (shard ^ 1) * height
    for b in range(row_blocks):
        start(
            other_ref.at[:, pl.ds(o_off + b * cols, cols)],
            buf.at[pl.ds(base + b * rows, rows), :],
            1,
        )
    for j, kz in enumerate(z_off):
        for k, (lo, hi) in enumerate(((low, high), (clow, chigh))):
            row0 = (shard ^ (2 * kz + k)) * height
            for i, kr in enumerate(r_off):
                src = lo if i < half else hi
                p = rep ^ kr
                block, col = (0, p) if row_blocks == 1 else (p // per, p % per)
                start(
                    src.at[i % half, j, :, pl.ds(off, n)],
                    buf.at[pl.ds(row0 + block * rows, rows), pl.ds(col * n, n)],
                    2 + 2 * j + k,
                )
    for at in range(2 + 2 * len(z_off)):
        flip = at if at < 2 else 2 * z_off[(at - 2) // 2] + at % 2
        area = pl.ds((shard ^ flip) * height, height)
        pltpu.make_async_copy(buf.at[area, :], buf.at[area, :], in_sem.at[at]).wait()
        pltpu.make_async_copy(buf.at[area, :], out_ref.at[area, :], out_sem).start()
    pltpu.make_async_copy(buf, out_ref, out_sem).wait()


def assemble(me, local, other, low, high, clow, chigh, n_shard, spec):
    layer, rows, cols, n, off, row_blocks, z_off, r_off, o_off = spec
    any_spec = pl.BlockSpec(memory_space=pl.ANY)
    shape = (n_shard * rows * row_blocks, cols)
    return pl.pallas_call(
        functools.partial(assemble_kernel, spec=spec),
        out_shape=jax.ShapeDtypeStruct(shape, jnp.bfloat16),
        in_specs=[pl.BlockSpec(memory_space=pltpu.SMEM)] + [any_spec] * 6,
        out_specs=any_spec,
        scratch_shapes=[
            pltpu.VMEM(shape, jnp.bfloat16),
            pltpu.SemaphoreType.DMA((n_shard,)),
            pltpu.SemaphoreType.DMA,
        ],
    )(me, local, other, low, high, clow, chigh)


def ffin_kernel(x_ref, w_ref, b_ref, act_ref, slope_ref):
    inner = jnp.dot(x_ref[...], w_ref[...], preferred_element_type=jnp.float32)
    inner = inner + b_ref[...].astype(jnp.float32)
    phi_big = 0.5 * (1.0 + lax.erf(inner * math.sqrt(0.5)))
    density = jnp.exp(-0.5 * inner * inner) * (1.0 / math.sqrt(2.0 * math.pi))
    act_ref[...] = (inner * phi_big).astype(jnp.bfloat16)
    slope_ref[...] = (phi_big + inner * density).astype(jnp.bfloat16)


def ffin_call(x, w, b, tile=512):
    rows, width = x.shape
    wide = w.shape[1]
    out = jax.ShapeDtypeStruct((rows, wide), jnp.bfloat16)
    return pl.pallas_call(
        ffin_kernel,
        grid=(wide // tile,),
        out_shape=(out, out),
        in_specs=[
            pl.BlockSpec((rows, width), lambda i: (0, 0)),
            pl.BlockSpec((width, tile), lambda i: (0, i)),
            pl.BlockSpec((1, tile), lambda i: (0, i)),
        ],
        out_specs=(pl.BlockSpec((rows, tile), lambda i: (0, i)),) * 2,
    )(x, w, b.reshape(1, wide))


def dot_rows(left, right):
    return lax.dot_general(
        left, right, (((0,), (0,)), ((), ())), preferred_element_type=jnp.float32
    )


def other_kernel(me_ref, left_ref, right_ref, out_ref):
    out_ref[0] = dot_rows(left_ref[...], right_ref[...]).astype(jnp.bfloat16)


def own_kernel(me_ref, left_ref, right_ref, came_ref, keep_ref, send_ref, *, half):
    bit = me_ref[2]
    left = left_ref[...]
    for target, at in ((keep_ref, bit), (send_ref, 1 - bit)):
        area = pl.ds(pl.multiple_of(at * half, 128), half)
        total = dot_rows(left, right_ref[:, area]) + came_ref[0, :, area].astype(jnp.float32)
        target[0] = total.astype(jnp.bfloat16)


def other_rows(me, left, right, n_shard):
    tokens, depth = left.shape
    height, wide, n_z = depth // n_shard, right.shape[1], n_shard // 2
    if height % 128:
        full = contract_rows(left, right).astype(jnp.bfloat16)
        return lax.dynamic_index_in_dim(
            full.reshape(n_z, 2, height, wide), 1 - me[1] % 2, axis=1, keepdims=False
        )
    return pl.pallas_call(
        other_kernel,
        grid_spec=pltpu.PrefetchScalarGridSpec(
            num_scalar_prefetch=1,
            grid=(n_z,),
            in_specs=[
                pl.BlockSpec((tokens, height), lambda i, m: (0, 2 * i + 1 - m[3])),
                pl.BlockSpec((tokens, wide), lambda i, m: (0, 0)),
            ],
            out_specs=pl.BlockSpec((1, height, wide), lambda i, m: (i, 0, 0)),
        ),
        out_shape=jax.ShapeDtypeStruct((n_z, height, wide), jnp.bfloat16),
    )(me, left, right)


def own_rows(me, left, right, came, n_shard, bit):
    tokens, depth = left.shape
    height, wide, n_z = depth // n_shard, right.shape[1], n_shard // 2
    half = wide // 2
    side = (me[0] // bit) % 2
    if height % 128:
        full = contract_rows(left, right)
        full = lax.dynamic_index_in_dim(
            full.reshape(n_z, 2, height, wide), me[1] % 2, axis=1, keepdims=False
        )
        full = (full + came.astype(jnp.float32)).astype(jnp.bfloat16)
        return split_columns(full, side)
    scalars = jnp.stack([me[0], me[1], side, me[3]])
    piece = jax.ShapeDtypeStruct((n_z, height, half), jnp.bfloat16)
    return pl.pallas_call(
        functools.partial(own_kernel, half=half),
        grid_spec=pltpu.PrefetchScalarGridSpec(
            num_scalar_prefetch=1,
            grid=(n_z,),
            in_specs=[
                pl.BlockSpec((tokens, height), lambda i, m: (0, 2 * i + m[3])),
                pl.BlockSpec((tokens, wide), lambda i, m: (0, 0)),
                pl.BlockSpec((1, height, wide), lambda i, m: (i, 0, 0)),
            ],
            out_specs=(pl.BlockSpec((1, height, half), lambda i, m: (i, 0, 0)),) * 2,
        ),
        out_shape=(piece, piece),
    )(scalars, left, right, came)


def split_columns(value, side):
    half = value.shape[-1] // 2
    take = lambda at: lax.dynamic_slice_in_dim(value, at * half, half, axis=value.ndim - 1)
    return take(side), take(1 - side)


def add_low(left, right):
    return (left.astype(jnp.float32) + right.astype(jnp.float32)).astype(jnp.bfloat16)


def reduce_rep(keep, send, me, n_rep, order):
    for at, bit in enumerate(order):
        if at:
            keep, send = split_columns(keep, (me[0] // bit) % 2)
        keep = add_low(keep, swap_rep(send, bit, n_rep))
    return keep


def reduce_z(pieces, me, n_shard):
    for bit in bits_of(n_shard)[1:]:
        side = (me[1] // bit) % 2
        pair = pieces.reshape((pieces.shape[0] // 2, 2) + pieces.shape[1:])
        take = lambda at: lax.dynamic_index_in_dim(pair, at, axis=1, keepdims=False)
        pieces = add_low(take(side), swap_shard(take(1 - side), bit, n_shard))
    return pieces[0]


def share_rep(piece, n_rep):
    have = piece[None]
    for bit in bits_of(n_rep):
        have = jnp.concatenate([have, swap_rep(have, bit, n_rep)])
    return have


def block_of(rep, order):
    block = 0
    for bit in order:
        block = block * 2 + (rep // bit) % 2
    return block


def place_columns(shared, off, n, rep, order):
    n_rep, rows = shared.shape[0], shared.shape[1]
    mine = block_of(rep, order)
    whole = jnp.zeros((rows, n_rep * n), jnp.float32)
    for k in range(n_rep):
        part = shared[k, :, off : off + n].astype(jnp.float32)
        whole = lax.dynamic_update_slice(whole, part, (0, (mine ^ block_of(k, order)) * n))
    return whole


def dot_low(left, right):
    return jnp.dot(left, right, preferred_element_type=jnp.float32).astype(jnp.bfloat16)


def forward_layer(hidden, weights, small, visible, heads):
    qkv_w, out_w, ffin_w, ffout_w = weights
    qv_b, out_b, gain_one, shift_one, ffin_b, ffout_b, gain_two, shift_two = small
    width = hidden.shape[1]
    rows = hidden.shape[0]
    hidden_b = hidden.astype(jnp.bfloat16)
    bias_full = jnp.concatenate(
        [qv_b[:width], jnp.zeros((width,), jnp.bfloat16), qv_b[width:]]
    ).astype(jnp.float32)
    qkv_rows = (product(hidden_b, qkv_w) + bias_full).astype(jnp.bfloat16)
    queries, key_rows, value_rows = head_blocks(qkv_rows, width, heads)
    scale = 1.0 / math.sqrt(queries.shape[2])
    scores = masked_scores(queries, key_rows, visible, scale)
    peak = jnp.max(scores, axis=-1, keepdims=True)
    expo = jnp.exp(scores - peak)
    total = jnp.sum(expo, axis=-1, keepdims=True)
    probs_b = (expo / total).astype(jnp.bfloat16)
    log_total = peak + jnp.log(total)
    mixed = jnp.einsum("hqk,khd->qhd", probs_b, value_rows, preferred_element_type=jnp.float32)
    mixed = mixed.reshape(rows, width).astype(jnp.bfloat16)
    resid_one = hidden + product(mixed, out_w) + out_b.astype(jnp.float32)
    first = layer_norm(resid_one, gain_one.astype(jnp.float32), shift_one.astype(jnp.float32))
    first_b = first.astype(jnp.bfloat16)
    active, slope = ffin_call(first_b, ffin_w, ffin_b)
    resid_two = first + product(active, ffout_w) + ffout_b.astype(jnp.float32)
    output = layer_norm(resid_two, gain_two.astype(jnp.float32), shift_two.astype(jnp.float32))
    kept = (hidden_b, qkv_rows, log_total, mixed, resid_one, first_b, slope, active, resid_two)
    return (output, kept)


def backward_layer(grad_out, weights, small, kept, visible, heads, reduce_weight):
    qkv_w, out_w, ffin_w, ffout_w = weights
    qv_b, out_b, gain_one, shift_one, ffin_b, ffout_b, gain_two, shift_two = small
    hidden_b, qkv_rows, log_total, mixed, resid_one, first_b, slope, active, resid_two = kept
    width = hidden_b.shape[1]
    rows = hidden_b.shape[0]
    _, pull_two = jax.vjp(
        layer_norm, resid_two, gain_two.astype(jnp.float32), shift_two.astype(jnp.float32)
    )
    grad_two, grad_gain_two, grad_shift_two = pull_two(grad_out)
    down_b = grad_two.astype(jnp.bfloat16)
    grad_ffout_bias = column_sums(down_b)
    reduce_weight("ffout", left=active, right=down_b)
    grad_inner = times_transposed(down_b, ffout_w) * slope.astype(jnp.float32)
    grad_inner = grad_inner.astype(jnp.bfloat16)
    grad_ffin_bias = column_sums(grad_inner)
    reduce_weight("ffin", left=first_b, right=grad_inner)
    grad_first = grad_two + times_transposed(grad_inner, ffin_w)
    _, pull_one = jax.vjp(
        layer_norm, resid_one, gain_one.astype(jnp.float32), shift_one.astype(jnp.float32)
    )
    grad_one, grad_gain_one, grad_shift_one = pull_one(grad_first)
    attn_grad = grad_one.astype(jnp.bfloat16)
    grad_out_bias = column_sums(attn_grad)
    reduce_weight("out", left=mixed, right=attn_grad)
    grad_mixed = times_transposed(attn_grad, out_w).astype(jnp.bfloat16)
    queries, key_rows, value_rows = head_blocks(qkv_rows, width, heads)
    scale = 1.0 / math.sqrt(queries.shape[2])
    scores = masked_scores(queries, key_rows, visible, scale)
    probs = jnp.exp(scores - log_total)
    probs_b = probs.astype(jnp.bfloat16)
    grad_heads = split_heads(grad_mixed, heads)
    grad_values = jnp.einsum(
        "hqk,qhd->khd", probs_b, grad_heads, preferred_element_type=jnp.float32
    )
    grad_probs = jnp.einsum(
        "qhd,khd->hqk", grad_heads, value_rows, preferred_element_type=jnp.float32
    )
    centre = jnp.sum(probs * grad_probs, axis=-1, keepdims=True)
    grad_scores = (probs * (grad_probs - centre)).astype(jnp.bfloat16)
    grad_queries = (
        jnp.einsum("hqk,khd->qhd", grad_scores, key_rows, preferred_element_type=jnp.float32)
        * scale
    )
    grad_keys = (
        jnp.einsum("hqk,qhd->khd", grad_scores, queries, preferred_element_type=jnp.float32) * scale
    )
    grad_qkv = jnp.concatenate(
        [
            grad_queries.reshape(rows, width),
            grad_keys.reshape(rows, width),
            grad_values.reshape(rows, width),
        ],
        axis=1,
    ).astype(jnp.bfloat16)
    grad_qv_bias = jnp.concatenate(
        [column_sums(grad_qkv[:, :width]), column_sums(grad_qkv[:, 2 * width :])]
    )
    reduce_weight("qkv", left=hidden_b, right=grad_qkv)
    grad_hidden = grad_one + times_transposed(grad_qkv, qkv_w)
    grads = (
        grad_qv_bias,
        grad_out_bias,
        grad_gain_one,
        grad_shift_one,
        grad_ffin_bias,
        grad_ffout_bias,
        grad_gain_two,
        grad_shift_two,
    )
    return (grad_hidden, grads)


def per_device(
    tokens,
    time_features,
    out_grad,
    deal,
    seq_lengths,
    seq_offsets,
    time_weight,
    time_bias,
    qkv_weight,
    qv_bias,
    out_weight,
    out_bias,
    norm1_gain,
    norm1_bias,
    ffin_weight,
    ffin_bias,
    ffout_weight,
    ffout_bias,
    norm2_gain,
    norm2_bias,
    *,
    n_rep,
    n_shard,
):
    heads = HEADS
    rep, shard = lax.axis_index("rep"), lax.axis_index("shard")
    me = jnp.stack([rep, shard, jnp.zeros_like(rep), shard % 2]).astype(jnp.int32)
    rows, width = tokens.shape
    R = qkv_weight.shape[1]
    up, down = bits_of(n_rep), bits_of(n_rep)[::-1]

    small_args = (
        qv_bias,
        out_bias,
        norm1_gain,
        norm1_bias,
        ffin_bias,
        ffout_bias,
        norm2_gain,
        norm2_bias,
    )
    flat = jnp.concatenate([time_bias] + [v.reshape(-1) for v in small_args])
    flat = jnp.pad(flat, (0, SMALL_ROWS * width - flat.shape[0])).reshape(SMALL_ROWS, width)
    time_ext = jnp.concatenate([time_weight, flat])

    mine = lax.dynamic_slice_in_dim(deal, shard * rows, rows)
    send_rank = jnp.sum((mine[None, :] < mine[:, None]).astype(jnp.int32), axis=1)
    slots = jnp.arange(rows, dtype=jnp.int32)
    send_mat = (send_rank[None, :] == slots[:, None]).astype(jnp.bfloat16)
    given = jnp.arange(deal.shape[0], dtype=jnp.int32)
    hit = deal[:, None] == (shard * rows + slots)[None, :]
    source = jnp.sum(jnp.where(hit, (given // rows)[:, None], 0), axis=0)
    key = source * rows + slots
    place = jnp.sum((key[None, :] < key[:, None]).astype(jnp.int32), axis=1)
    place_mat = (place[:, None] == slots[None, :]).astype(jnp.bfloat16)

    def exchange(value):
        return lax.all_to_all(value, "shard", split_axis=0, concat_axis=0, tiled=True)

    came = exchange(dot_low(send_mat, jnp.concatenate([tokens, time_features], axis=1)))
    dealt = dot_low(place_mat, came)
    dealt_tokens, dealt_features = dealt[:, :width], dealt[:, width:]

    starts = seq_offsets[0][:, None]
    finish = starts + seq_lengths[0][:, None]
    member = (slots[None, :] >= starts) & (slots[None, :] < finish)
    visible = jnp.any(member[:, :, None] & member[:, None, :], axis=0) | (
        slots[:, None] == slots[None, :]
    )

    arrays = {
        "qkv": (qkv_weight, 1),
        "out": (out_weight, 1),
        "ffin": (ffin_weight, 1),
        "ffout": (ffout_weight, ffout_weight.shape[1] // R),
    }

    def rep_slice(array, layer, blocks):
        if blocks == 1:
            n = array.shape[2] // n_rep
            return lax.dynamic_slice(array, (layer, 0, rep * n), (1, R, n))[0]
        per = n_rep // blocks
        n = array.shape[2] // per
        return lax.dynamic_slice(
            array, (layer, (rep // per) * R, (rep % per) * n), (1, R, n)
        )[0]

    own_parts, own_off, at = [], {}, 0
    for layer in range(LAYERS):
        for name, (array, blocks) in arrays.items():
            own_off[name, layer] = at
            for b in range(blocks):
                own_parts.append(array[layer, b * R : (b + 1) * R])
                at += array.shape[2]
    time_other = swap_shard(time_ext, 1, n_shard)
    other = swap_shard(jnp.concatenate(own_parts, axis=1), 1, n_shard)
    me2 = jnp.stack([rep, shard]).astype(jnp.int32)

    def group(members, order):
        pieces = [rep_slice(arrays[name][0], layer, arrays[name][1]) for name, layer in members]
        z_pieces, z_off = gather_z(jnp.concatenate(pieces, axis=1), n_shard)
        low, high, r_off = gather_rep(z_pieces, n_rep, order)
        clow, chigh = swap_shard(low, 1, n_shard), swap_shard(high, 1, n_shard)
        off = 0
        for (name, layer), piece in zip(members, pieces):
            array, blocks = arrays[name]
            spec = (
                layer,
                R,
                array.shape[2],
                piece.shape[1],
                off,
                blocks,
                tuple(z_off),
                tuple(r_off),
                own_off[name, layer],
            )
            off += piece.shape[1]
            full[name, layer] = assemble(
                me2, array, other, low, high, clow, chigh, n_shard, spec
            )

    full = {}
    n_time = width // n_rep
    z_pieces, z_off = gather_z(
        lax.dynamic_slice_in_dim(time_ext, rep * n_time, n_time, axis=1), n_shard
    )
    low, high, r_off = gather_rep(z_pieces, n_rep, up)
    clow, chigh = swap_shard(low, 1, n_shard), swap_shard(high, 1, n_shard)
    time_rows = R + SMALL_ROWS
    spec = (None, time_rows, width, n_time, 0, 1, tuple(z_off), tuple(r_off), 0)
    time_all = assemble(me2, time_ext, time_other, low, high, clow, chigh, n_shard, spec)
    time_all = time_all.reshape(n_shard, time_rows, width)
    time_full = time_all[:, :R].reshape(n_shard * R, width)
    small_all = time_all[:, R:].reshape(n_shard, SMALL_ROWS * width)
    group([("qkv", 0), ("out", 0)], down)
    group([("ffin", 0)], up)
    group([("ffout", 0)], down)
    group([("qkv", 1), ("out", 1)], up)
    group([("ffin", 1)], down)
    group([("ffout", 1)], up)

    at = time_bias.shape[0]
    time_shift = small_all[:, :at].reshape(-1)
    vectors = []
    for v in small_args:
        n = v.shape[1]
        vectors.append(
            [small_all[:, at + k * n : at + (k + 1) * n].reshape(-1) for k in range(LAYERS)]
        )
        at += LAYERS * n

    hidden = (
        dealt_tokens.astype(jnp.float32)
        + product(dealt_features, time_full)
        + time_shift.astype(jnp.float32)
    )
    kept_all = []
    for layer in range(LAYERS):
        small = [v[layer] for v in vectors]
        weights = [full[name, layer] for name in ("qkv", "out", "ffin", "ffout")]
        hidden, kept = forward_layer(hidden, weights, small, visible, heads)
        kept_all.append(kept)

    dealt_cot = dot_low(place_mat, exchange(dot_low(send_mat, out_grad)))
    hidden_out = dot_rows(place_mat, hidden.astype(jnp.bfloat16)).astype(jnp.bfloat16)
    home_hidden = dot_rows(send_mat, exchange(hidden_out)).astype(jnp.bfloat16)

    reduced, small_grads = {}, {}
    orders = {"ffout": up, "ffin": down, "out": up, "qkv": down}

    def reduce_weight(name, layer, left, right):
        order = orders[name] if layer == 1 else orders[name]
        came_rows = swap_shard(other_rows(me, left, right, n_shard), 1, n_shard)
        keep, send = own_rows(me, left, right, came_rows, n_shard, order[0])
        reduced[name, layer] = reduce_rep(keep, send, me, n_rep, order)

    def finish(names):
        pieces, spans, at = [], {}, 0
        for key in names:
            piece = reduced[key]
            blocks = piece.shape[1] // R if piece.shape[1] % R == 0 else 1
            n = piece.shape[2]
            spans[key] = (at, n, blocks)
            for b in range(blocks):
                pieces.append(piece[:, b * R : (b + 1) * R] if blocks > 1 else piece)
                at += n
        shared = share_rep(reduce_z(jnp.concatenate(pieces, axis=2), me, n_shard), n_rep)
        for key, (at, n, blocks) in spans.items():
            parts = [
                place_columns(shared, at + b * n, n, rep, orders[key[0]]) for b in range(blocks)
            ]
            final[key] = parts[0] if blocks == 1 else jnp.concatenate(parts)

    final = {}
    grad_hidden = dealt_cot.astype(jnp.float32)
    for layer in reversed(range(LAYERS)):
        small = [v[layer] for v in vectors]
        weights = [full[name, layer] for name in ("qkv", "out", "ffin", "ffout")]
        grad_hidden, small_grads[layer] = backward_layer(
            grad_hidden,
            weights,
            small,
            kept_all[layer],
            visible,
            heads,
            functools.partial(reduce_weight, layer=layer),
        )
        finish([("ffout", layer), ("ffin", layer)])
        finish([("out", layer), ("qkv", layer)])

    grad_embed = grad_hidden.astype(jnp.bfloat16)
    home_grad = dot_rows(
        send_mat, exchange(dot_rows(place_mat, grad_embed).astype(jnp.bfloat16))
    ).astype(jnp.bfloat16)

    spread = [column_sums(grad_embed).reshape(n_shard, -1)]
    for k in range(len(small_args)):
        for layer in range(LAYERS):
            spread.append(small_grads[layer][k].reshape(n_shard, -1))
    spread = jnp.concatenate(spread, axis=1)
    used = spread.shape[1]
    spread = jnp.pad(spread, ((0, 0), (0, SMALL_ROWS * width - used)))
    n_z = n_shard // 2
    time_grad = contract_rows(dealt_features, grad_embed).reshape(n_z, 2, R, width)
    time_grad = jnp.concatenate(
        [time_grad, spread.reshape(n_z, 2, SMALL_ROWS, width)], axis=2
    ).astype(jnp.bfloat16)
    core = shard % 2
    pick = lambda at: lax.dynamic_index_in_dim(time_grad, at, axis=1, keepdims=False)
    pair = add_low(pick(core), swap_shard(pick(1 - core), 1, n_shard))
    keep, send = split_columns(pair, (rep // up[0]) % 2)
    time_sum = reduce_z(reduce_rep(keep, send, me, n_rep, up), me, n_shard)
    time_sum = place_columns(share_rep(time_sum, n_rep), 0, n_time, rep, up)
    time_w_grad = time_sum[:R]
    small_sum = time_sum[R:].reshape(-1)
    at = time_bias.shape[0]
    time_b_grad = small_sum[:at]
    small_out = []
    for v in small_args:
        n = LAYERS * v.shape[1]
        small_out.append(small_sum[at : at + n].reshape(LAYERS, -1))
        at += n
    stack = {name: jnp.stack([final[name, k] for k in range(LAYERS)]) for name in arrays}
    return (
        home_hidden,
        home_grad,
        time_w_grad,
        time_b_grad,
        stack["qkv"],
        small_out[0],
        stack["out"],
        small_out[1],
        small_out[2],
        small_out[3],
        stack["ffin"],
        small_out[4],
        stack["ffout"],
        small_out[5],
        small_out[6],
        small_out[7],
    )


def solution(mesh):
    in_specs = (
        P(("rep", "shard"), None),
        P(("rep", "shard"), None),
        P(("rep", "shard"), None),
        P("rep"),
        P(("rep", "shard"), None),
        P(("rep", "shard"), None),
        P("shard", None),
        P("shard"),
        P(None, "shard", None),
        P(None, "shard"),
        P(None, "shard", None),
        P(None, "shard"),
        P(None, "shard"),
        P(None, "shard"),
        P(None, "shard", None),
        P(None, "shard"),
        P(None, "shard", None),
        P(None, "shard"),
        P(None, "shard"),
        P(None, "shard"),
    )
    out_specs = (
        P(("rep", "shard"), None),
        P(("rep", "shard"), None),
        P("shard", None),
        P("shard"),
        P(None, "shard", None),
        P(None, "shard"),
        P(None, "shard", None),
        P(None, "shard"),
        P(None, "shard"),
        P(None, "shard"),
        P(None, "shard", None),
        P(None, "shard"),
        P(None, "shard", None),
        P(None, "shard"),
        P(None, "shard"),
        P(None, "shard"),
    )
    body = functools.partial(
        per_device, n_rep=mesh.shape["rep"], n_shard=mesh.shape["shard"]
    )
    return jax.shard_map(
        body, mesh=mesh, in_specs=in_specs, out_specs=out_specs, check_vma=False
    )
```

```python
import functools
import math

import jax
import jax.numpy as jnp
from jax import lax
from jax.experimental import pallas as pl
from jax.experimental.pallas import tpu as pltpu
from jax.sharding import PartitionSpec as P

HEADS = 16
LAYERS = 2
SMALL_ROWS = 16


epsilon = 1e-05
negative = -1e30

def layer_norm(values, gain, shift):
    centred = values - jnp.mean(values, axis=-1, keepdims=True)
    spread = jnp.mean(centred * centred, axis=-1, keepdims=True)
    return centred * lax.rsqrt(spread + epsilon) * gain + shift


def product(left, right):
    return jnp.dot(left, right, preferred_element_type=jnp.float32)


def contract_rows(left, right):
    return lax.dot_general(
        left, right, (((0,), (0,)), ((), ())), preferred_element_type=jnp.float32
    )


def times_transposed(left, right):
    return lax.dot_general(
        left, right, (((1,), (1,)), ((), ())), preferred_element_type=jnp.float32
    )


def column_sums(values):
    return jnp.sum(values.astype(jnp.float32), axis=0)


def bits_of(count):
    return [1 << k for k in range(count.bit_length() - 1)]


def swap_rep(value, bit, n_rep):
    return lax.ppermute(value, "rep", [(i, i ^ bit) for i in range(n_rep)])


def swap_shard(value, bit, n_shard):
    return lax.ppermute(value, "shard", [(i, i ^ bit) for i in range(n_shard)])


def gather_chunk(pieces, n_rep, n_shard, lanes, box):
    have = pieces = jnp.concatenate(pieces, axis=1)[None] if len(pieces) > 1 else pieces[0][None]
    parts = []
    for bit in bits_of(n_shard)[1:][::-1]:
        got = yield (have, swap_shard(have, bit, n_shard))
        parts.append(got[1])
        have = jnp.concatenate([got[0], got[1]])
    n = pieces.shape[2] // len(lanes)
    cut = lambda v, k: v[:, :, k * n : (k + 1) * n]
    have = [jnp.concatenate([cut(v, k) for v in parts])[None] for k in range(len(lanes))]
    for at in range(len(lanes[0])):
        last = at == len(lanes[0]) - 1
        sent = [swap_rep(v, order[at], n_rep) for v, order in zip(have, lanes)]
        core = [swap_shard(v, 1, n_shard) for v in have] if last else []
        have, sent, core = yield (have, sent, core)
        if not last:
            have = [jnp.concatenate([v, w]) for v, w in zip(have, sent)]
    have, sent, core, high = yield (
        have,
        sent,
        core,
        [swap_shard(v, 1, n_shard) for v in sent],
    )
    box.extend(zip(have, sent, core, high))


def offsets_of(bits):
    offsets = [0]
    for bit in bits:
        offsets = offsets + [o ^ bit for o in offsets]
    return tuple(offsets)


class Flow:
    def __init__(self):
        self.live = []

    def add(self, stages):
        self.live.append((stages, next(stages)))

    def until(self, done, state):
        while not done():
            state = self.step(state)
        return state

    def step(self, state):
        values, state = lax.optimization_barrier(([v for _, v in self.live], state))
        before, self.live = self.live, []
        for (stages, _), value in zip(before, values):
            try:
                self.live.append((stages, stages.send(value)))
            except StopIteration:
                pass
        return state


def assemble_kernel(me_ref, local_ref, other_ref, *refs, spec):
    out_ref, buf, in_sem, out_sem = refs[-4:]
    layer, rows, cols, row_blocks, o_off, z_off, r_offs, segments = spec
    rep, shard = me_ref[0], me_ref[1]
    local = local_ref if layer is None else local_ref.at[layer]
    height = rows * row_blocks
    n = sum(seg[2] for seg in segments)
    per = cols // n

    def start(src, dst, at):
        pltpu.make_async_copy(src, dst, in_sem.at[at]).start()

    start(local, buf.at[pl.ds(shard * height, height), :], 0)
    base = (shard ^ 1) * height
    for b in range(row_blocks):
        start(
            other_ref.at[:, pl.ds(o_off + b * cols, cols)],
            buf.at[pl.ds(base + b * rows, rows), :],
            1,
        )
    for j, kz in enumerate(z_off):
        for k in range(2):
            row0 = (shard ^ (2 * kz + k)) * height
            for lane, off, wide, col0 in segments:
                lo, hi = refs[4 * lane + 2 * k], refs[4 * lane + 2 * k + 1]
                half = len(r_offs[lane]) // 2
                for i, kr in enumerate(r_offs[lane]):
                    src = lo if i < half else hi
                    p = rep ^ kr
                    block, col = (0, p) if row_blocks == 1 else (p // per, p % per)
                    start(
                        src.at[i % half, j, :, pl.ds(off, wide)],
                        buf.at[
                            pl.ds(row0 + block * rows, rows), pl.ds(col * n + col0, wide)
                        ],
                        2 + 2 * j + k,
                    )
    for at in range(2 + 2 * len(z_off)):
        flip = at if at < 2 else 2 * z_off[(at - 2) // 2] + at % 2
        area = pl.ds((shard ^ flip) * height, height)
        pltpu.make_async_copy(buf.at[area, :], buf.at[area, :], in_sem.at[at]).wait()
        pltpu.make_async_copy(buf.at[area, :], out_ref.at[area, :], out_sem).start()
    pltpu.make_async_copy(buf, out_ref, out_sem).wait()


def assemble(me, local, other, box, n_shard, spec):
    layer, rows, cols, row_blocks = spec[:4]
    any_spec = pl.BlockSpec(memory_space=pl.ANY)
    shape = (n_shard * rows * row_blocks, cols)
    flat = [v for lane in box for v in (lane[0], lane[1], lane[2], lane[3])]
    return pl.pallas_call(
        functools.partial(assemble_kernel, spec=spec),
        out_shape=jax.ShapeDtypeStruct(shape, jnp.bfloat16),
        in_specs=[pl.BlockSpec(memory_space=pltpu.SMEM)] + [any_spec] * (2 + len(flat)),
        out_specs=any_spec,
        scratch_shapes=[
            pltpu.VMEM(shape, jnp.bfloat16),
            pltpu.SemaphoreType.DMA((n_shard,)),
            pltpu.SemaphoreType.DMA,
        ],
    )(me, local, other, *flat)


def ffin_kernel(x_ref, w_ref, b_ref, act_ref, slope_ref):
    inner = jnp.dot(x_ref[...], w_ref[...], preferred_element_type=jnp.float32)
    inner = inner + b_ref[...].astype(jnp.float32)
    phi_big = 0.5 * (1.0 + lax.erf(inner * math.sqrt(0.5)))
    density = jnp.exp(-0.5 * inner * inner) * (1.0 / math.sqrt(2.0 * math.pi))
    act_ref[...] = (inner * phi_big).astype(jnp.bfloat16)
    slope_ref[...] = (phi_big + inner * density).astype(jnp.bfloat16)


def ffin_call(x, w, b, tile=512):
    rows, width = x.shape
    wide = w.shape[1]
    out = jax.ShapeDtypeStruct((rows, wide), jnp.bfloat16)
    return pl.pallas_call(
        ffin_kernel,
        grid=(wide // tile,),
        out_shape=(out, out),
        in_specs=[
            pl.BlockSpec((rows, width), lambda i: (0, 0)),
            pl.BlockSpec((width, tile), lambda i: (0, i)),
            pl.BlockSpec((1, tile), lambda i: (0, i)),
        ],
        out_specs=(pl.BlockSpec((rows, tile), lambda i: (0, i)),) * 2,
    )(x, w, b.reshape(1, wide))


def dot_rows(left, right):
    return lax.dot_general(
        left, right, (((0,), (0,)), ((), ())), preferred_element_type=jnp.float32
    )


def other_kernel(me_ref, *refs):
    lefts, (right_ref, out_ref, turned) = refs[:-3], refs[-3:]
    height = out_ref.shape[1]

    @pl.when(pl.program_id(0) == 0)
    def _():
        for z, ref in enumerate(lefts):
            turned[z * height : (z + 1) * height, :] = ref[...].T

    total = product(turned[...], right_ref[...])
    out_ref[...] = total.reshape(out_ref.shape).astype(jnp.bfloat16)


def own_kernel(me_ref, *refs):
    lefts, (right_ref, came_ref), outs, turned = refs[:-7], refs[-7:-5], refs[-5:-1], refs[-1]
    height = came_ref.shape[1]
    step = pl.program_id(0)

    @pl.when(step == 0)
    def _():
        for z, ref in enumerate(lefts):
            turned[z * height : (z + 1) * height, :] = ref[...].T

    total = product(turned[...], right_ref[...]).reshape(came_ref.shape)
    total = (total + came_ref[...].astype(jnp.float32)).astype(jnp.bfloat16)
    for at, out_ref in enumerate(outs):

        @pl.when(step == at)
        def _():
            out_ref[...] = total


def other_rows(me, left, right, n_shard):
    tokens, depth = left.shape
    height, wide, n_z = depth // n_shard, right.shape[1], n_shard // 2
    if height % 128:
        full = contract_rows(left, right).astype(jnp.bfloat16)
        return lax.dynamic_index_in_dim(
            full.reshape(n_z, 2, height, wide), 1 - me[1] % 2, axis=1, keepdims=False
        )
    tile = wide // 4
    return pl.pallas_call(
        other_kernel,
        grid_spec=pltpu.PrefetchScalarGridSpec(
            num_scalar_prefetch=1,
            grid=(4,),
            in_specs=[
                pl.BlockSpec((tokens, height), lambda i, m, z=z: (0, 2 * z + 1 - m[3]))
                for z in range(n_z)
            ]
            + [pl.BlockSpec((tokens, tile), lambda i, m: (0, i))],
            out_specs=pl.BlockSpec((n_z, height, tile), lambda i, m: (0, 0, i)),
            scratch_shapes=[pltpu.VMEM((n_z * height, tokens), jnp.bfloat16)],
        ),
        out_shape=jax.ShapeDtypeStruct((n_z, height, wide), jnp.bfloat16),
    )(me, *([left] * n_z), right)


def own_rows(me, left, right, came, n_shard, bits):
    tokens, depth = left.shape
    height, wide, n_z = depth // n_shard, right.shape[1], n_shard // 2
    sides = [(me[0] // bit) % 2 for bit in bits]
    if height % 128:
        full = contract_rows(left, right)
        full = lax.dynamic_index_in_dim(
            full.reshape(n_z, 2, height, wide), me[1] % 2, axis=1, keepdims=False
        )
        full = (full + came.astype(jnp.float32)).astype(jnp.bfloat16)
        halves = (full[:, :, : wide // 2], full[:, :, wide // 2 :])
        return [split_columns(v, side) for v, side in zip(halves, sides)]
    tile = wide // 4
    scalars = jnp.stack([sides[0], 1 - sides[0], 2 + sides[1], 3 - sides[1], me[3]])
    piece = jax.ShapeDtypeStruct((n_z, height, tile), jnp.bfloat16)
    outs = pl.pallas_call(
        own_kernel,
        grid_spec=pltpu.PrefetchScalarGridSpec(
            num_scalar_prefetch=1,
            grid=(4,),
            in_specs=[
                pl.BlockSpec((tokens, height), lambda i, m, z=z: (0, 2 * z + m[4]))
                for z in range(n_z)
            ]
            + [
                pl.BlockSpec((tokens, tile), lambda i, m: (0, m[i])),
                pl.BlockSpec((n_z, height, tile), lambda i, m: (0, 0, m[i])),
            ],
            out_specs=(pl.BlockSpec((n_z, height, tile), lambda i, m: (0, 0, 0)),) * 4,
            scratch_shapes=[pltpu.VMEM((n_z * height, tokens), jnp.bfloat16)],
        ),
        out_shape=(piece,) * 4,
    )(scalars, *([left] * n_z), right, came)
    return [outs[:2], outs[2:]]


def split_columns(value, side):
    half = value.shape[-1] // 2
    take = lambda at: lax.dynamic_slice_in_dim(value, at * half, half, axis=value.ndim - 1)
    return take(side), take(1 - side)


def add_low(left, right):
    return (left.astype(jnp.float32) + right.astype(jnp.float32)).astype(jnp.bfloat16)


def block_of(rep, order):
    block = 0
    for bit in order:
        block = block * 2 + (rep // bit) % 2
    return block


def place_columns(shared, span, rep, orders):
    n_rep, rows = shared.shape[0], shared.shape[1]
    blocks = 1 + max(b for b, _, _, _ in span)
    lanes = 1 + max(lane for _, lane, _, _ in span)
    n = span[0][3]
    whole = jnp.zeros((blocks * rows, lanes * n_rep * n), jnp.float32)
    for b, lane, off, _ in span:
        mine = block_of(rep, orders[lane])
        for k in range(n_rep):
            part = shared[k, :, off : off + n].astype(jnp.float32)
            to = lane * n_rep + (mine ^ block_of(k, orders[lane]))
            whole = lax.dynamic_update_slice(whole, part, (b * rows, to * n))
    return whole


def dot_low(left, right):
    return jnp.dot(left, right, preferred_element_type=jnp.float32).astype(jnp.bfloat16)


def low_lanes(shape, size):
    return lax.broadcasted_iota(jnp.int32, shape, 1) < size


def attend_kernel(q_ref, k_ref, v_ref, hide_ref, out_ref, log_ref, *, size):
    first = low_lanes(q_ref.shape, size)
    q, k, v, hide = q_ref[...], k_ref[...], v_ref[...], hide_ref[...]
    mixed, logs = [], []
    for h in range(2):
        mine = jnp.where(first if h == 0 else ~first, q, jnp.zeros_like(q))
        scores = times_transposed(mine, k) * (1.0 / math.sqrt(size)) + hide
        peak = jnp.max(scores, axis=-1, keepdims=True)
        expo = jnp.exp(scores - peak)
        total = jnp.sum(expo, axis=-1, keepdims=True)
        mixed.append(product((expo * (1.0 / total)).astype(jnp.bfloat16), v))
        logs.append(peak + jnp.log(total))
    out_ref[...] = jnp.where(first, mixed[0], mixed[1]).astype(jnp.bfloat16)
    log_ref[...] = jnp.where(first, logs[0], logs[1])


def attend_call(qkv_rows, hide, heads):
    rows, width = qkv_rows.shape[0], qkv_rows.shape[1] // 3
    pairs = heads // 2
    wide = width // pairs
    part = lambda k: pl.BlockSpec((rows, wide), lambda i, k=k: (0, k * pairs + i))
    return pl.pallas_call(
        functools.partial(attend_kernel, size=width // heads),
        grid=(pairs,),
        in_specs=[part(0), part(1), part(2), pl.BlockSpec((rows, rows), lambda i: (0, 0))],
        out_specs=(part(0), part(0)),
        out_shape=(
            jax.ShapeDtypeStruct((rows, width), jnp.bfloat16),
            jax.ShapeDtypeStruct((rows, width), jnp.float32),
        ),
    )(qkv_rows, qkv_rows, qkv_rows, hide)


def attend_back_kernel(
    q_ref, k_ref, v_ref, hide_ref, log_ref, grad_ref, w_ref, out_ref, *, size, width
):
    at = pl.program_id(0)
    first = low_lanes(q_ref.shape, size)
    q, k, v, hide = q_ref[...], k_ref[...], v_ref[...], hide_ref[...]
    scale = 1.0 / math.sqrt(size)
    grad = times_transposed(grad_ref[...], w_ref[...]).astype(jnp.bfloat16)
    parts = []
    for h in range(2):
        side = first if h == 0 else ~first
        mine = jnp.where(side, q, jnp.zeros_like(q))
        gone = jnp.where(side, grad, jnp.zeros_like(grad))
        scores = times_transposed(mine, k) * scale + hide
        probs = jnp.exp(scores - log_ref[:, h * size : h * size + 1])
        pull = times_transposed(gone, v)
        centre = jnp.sum(probs * pull, axis=-1, keepdims=True)
        back = (probs * (pull - centre)).astype(jnp.bfloat16)
        parts.append(
            (
                product(back, k) * scale,
                contract_rows(back, q) * scale,
                contract_rows(probs.astype(jnp.bfloat16), grad),
            )
        )
    for m in range(3):
        area = pl.ds(pl.multiple_of(m * width + at * 2 * size, 128), 2 * size)
        out_ref[:, area] = jnp.where(first, parts[0][m], parts[1][m]).astype(jnp.bfloat16)


def attend_back(attn_grad, out_w, qkv_rows, logs, hide, heads):
    rows, width = attn_grad.shape
    pairs = heads // 2
    wide = width // pairs
    part = lambda k: pl.BlockSpec((rows, wide), lambda i, k=k: (0, k * pairs + i))
    return pl.pallas_call(
        functools.partial(attend_back_kernel, size=width // heads, width=width),
        grid=(pairs,),
        in_specs=[
            part(0),
            part(1),
            part(2),
            pl.BlockSpec((rows, rows), lambda i: (0, 0)),
            part(0),
            pl.BlockSpec((rows, width), lambda i: (0, 0)),
            pl.BlockSpec((wide, width), lambda i: (i, 0)),
        ],
        out_specs=pl.BlockSpec((rows, 3 * width), lambda i: (0, 0)),
        out_shape=jax.ShapeDtypeStruct((rows, 3 * width), jnp.bfloat16),
    )(qkv_rows, qkv_rows, qkv_rows, hide, logs, attn_grad, out_w)


def attend(hidden, qkv_w, out_w, small, hide, heads):
    qv_b, out_b, gain_one, shift_one = small[:4]
    width = hidden.shape[1]
    hidden_b = hidden.astype(jnp.bfloat16)
    bias_full = jnp.concatenate(
        [qv_b[:width], jnp.zeros((width,), jnp.bfloat16), qv_b[width:]]
    ).astype(jnp.float32)
    qkv_rows = (product(hidden_b, qkv_w) + bias_full).astype(jnp.bfloat16)
    mixed, logs = attend_call(qkv_rows, hide, heads)
    resid_one = hidden + product(mixed, out_w) + out_b.astype(jnp.float32)
    first = layer_norm(resid_one, gain_one.astype(jnp.float32), shift_one.astype(jnp.float32))
    return first, (hidden_b, qkv_rows, logs, mixed, resid_one, first.astype(jnp.bfloat16))


def feed_out(first, active, ffout_w, small):
    ffout_b, gain_two, shift_two = small[5:]
    resid_two = first + product(active, ffout_w) + ffout_b.astype(jnp.float32)
    output = layer_norm(resid_two, gain_two.astype(jnp.float32), shift_two.astype(jnp.float32))
    return output, resid_two


def norm_back(grad, resid, gain, shift):
    _, pull = jax.vjp(layer_norm, resid, gain.astype(jnp.float32), shift.astype(jnp.float32))
    return pull(grad)


def per_device(
    tokens,
    time_features,
    out_grad,
    deal,
    seq_lengths,
    seq_offsets,
    time_weight,
    time_bias,
    qkv_weight,
    qv_bias,
    out_weight,
    out_bias,
    norm1_gain,
    norm1_bias,
    ffin_weight,
    ffin_bias,
    ffout_weight,
    ffout_bias,
    norm2_gain,
    norm2_bias,
    *,
    n_rep,
    n_shard,
):
    heads = HEADS
    rep, shard = lax.axis_index("rep"), lax.axis_index("shard")
    me = jnp.stack([rep, shard, jnp.zeros_like(rep), shard % 2]).astype(jnp.int32)
    rows, width = tokens.shape
    R = qkv_weight.shape[1]
    up, down = bits_of(n_rep), bits_of(n_rep)[::-1]

    small_args = (
        qv_bias,
        out_bias,
        norm1_gain,
        norm1_bias,
        ffin_bias,
        ffout_bias,
        norm2_gain,
        norm2_bias,
    )
    flat = jnp.concatenate([time_bias] + [v.reshape(-1) for v in small_args])
    flat = jnp.pad(flat, (0, SMALL_ROWS * width - flat.shape[0])).reshape(SMALL_ROWS, width)
    time_ext = jnp.concatenate([time_weight, flat])

    mine = lax.dynamic_slice_in_dim(deal, shard * rows, rows)
    send_rank = jnp.sum((mine[None, :] < mine[:, None]).astype(jnp.int32), axis=1)
    slots = jnp.arange(rows, dtype=jnp.int32)
    send_mat = (send_rank[None, :] == slots[:, None]).astype(jnp.bfloat16)
    given = jnp.arange(deal.shape[0], dtype=jnp.int32)
    hit = deal[:, None] == (shard * rows + slots)[None, :]
    source = jnp.sum(jnp.where(hit, (given // rows)[:, None], 0), axis=0)
    key = source * rows + slots
    place = jnp.sum((key[None, :] < key[:, None]).astype(jnp.int32), axis=1)
    place_mat = (place[:, None] == slots[None, :]).astype(jnp.bfloat16)

    def exchange(value):
        return lax.all_to_all(value, "shard", split_axis=0, concat_axis=0, tiled=True)

    starts = seq_offsets[0][:, None]
    finish = starts + seq_lengths[0][:, None]
    member = (slots[None, :] >= starts) & (slots[None, :] < finish)
    visible = jnp.any(member[:, :, None] & member[:, None, :], axis=0) | (
        slots[:, None] == slots[None, :]
    )
    hide = jnp.where(visible, 0.0, negative).astype(jnp.float32)

    names = ("qkv", "out", "ffin", "ffout")
    arrays = {
        "qkv": (qkv_weight, 1),
        "out": (out_weight, 1),
        "ffin": (ffin_weight, 1),
        "ffout": (ffout_weight, ffout_weight.shape[1] // R),
    }
    time_rows = R + SMALL_ROWS
    z_off = tuple(o >> 1 for o in offsets_of(bits_of(n_shard)[1:][::-1]))[1:]
    me2 = jnp.stack([rep, shard]).astype(jnp.int32)
    own_parts, own_off, at = [], {}, 0
    for layer in range(LAYERS):
        for name in names:
            array, blocks = arrays[name]
            own_off[name, layer] = at
            for b in range(blocks):
                own_parts.append(array[layer, b * R : (b + 1) * R])
                at += array.shape[2]

    def rep_slice(array, layer, blocks):
        if blocks == 1:
            n = array.shape[2] // n_rep
            return lax.dynamic_slice(array, (layer, 0, rep * n), (1, R, n))[0]
        per = n_rep // blocks
        n = array.shape[2] // per
        return lax.dynamic_slice(
            array, (layer, (rep // per) * R, (rep % per) * n), (1, R, n)
        )[0]

    flow = Flow()
    boxes = {}

    def gather_weights(members, raw):
        pieces = [rep_slice(raw[name], layer, arrays[name][1]) for name, layer in members]
        box, lanes = [], (up, down)
        wide = sum(p.shape[1] for p in pieces) // 2
        at = 0
        for (name, layer), piece in zip(members, pieces):
            n, segments, col = piece.shape[1], [], 0
            while col < n:
                lane, off = divmod(at, wide)
                size = min(n - col, wide - off)
                segments.append((lane, off, size, col))
                at, col = at + size, col + size
            boxes[name, layer] = (box, tuple(segments))
        flow.add(gather_chunk(pieces, n_rep, n_shard, lanes, box))

    def whole_weight(name, layer):
        array, blocks = arrays[name]
        box, segments = boxes[name, layer]
        spec = (
            layer,
            R,
            array.shape[2],
            blocks,
            own_off[name, layer],
            z_off,
            (offsets_of(up), offsets_of(down)),
            segments,
        )
        return assemble(me2, array, other, box, n_shard, spec)

    raw = {name: arrays[name][0] for name in names}
    n_time = width // n_rep
    time_box = []
    time_piece = lax.dynamic_slice_in_dim(time_ext, rep * n_time, n_time, axis=1)
    flow.add(gather_chunk([time_piece], n_rep, n_shard, (up,), time_box))
    time_other = swap_shard(time_ext, 1, n_shard)
    raw, time_other, cot = flow.step((raw, time_other, out_grad))
    gather_weights([("qkv", 0), ("out", 0)], raw)
    came = exchange(dot_low(send_mat, jnp.concatenate([tokens, time_features], axis=1)))
    raw, came = flow.step((raw, came))
    gather_weights([("ffin", 0)], raw)
    dealt = dot_low(place_mat, came)
    dealt_tokens, dealt_features = dealt[:, :width], dealt[:, width:]
    raw, dealt_tokens, dealt_features, cot = flow.step((raw, dealt_tokens, dealt_features, cot))
    gather_weights([("ffout", 0)], raw)
    came_cot = exchange(dot_low(send_mat, cot))
    other = swap_shard(jnp.concatenate(own_parts, axis=1), 1, n_shard)
    raw, came_cot, other = flow.step((raw, came_cot, other))
    gather_weights([("qkv", 1), ("out", 1)], raw)
    dealt_cot = dot_low(place_mat, came_cot)
    raw, dealt_cot = flow.step((raw, dealt_cot))
    gather_weights([("ffin", 1)], raw)
    raw = flow.until(lambda: time_box, raw)

    spec = (
        None,
        time_rows,
        width,
        1,
        0,
        z_off,
        (offsets_of(up),),
        ((0, 0, n_time, 0),),
    )
    time_all = assemble(me2, time_ext, time_other, time_box, n_shard, spec)
    time_all = time_all.reshape(n_shard, time_rows, width)
    time_full = time_all[:, :R].reshape(n_shard * R, width)
    small_all = time_all[:, R:].reshape(n_shard, SMALL_ROWS * width)
    at = time_bias.shape[0]
    time_shift = small_all[:, :at].reshape(-1)
    vectors = []
    for v in small_args:
        n = v.shape[1]
        vectors.append(
            [small_all[:, at + k * n : at + (k + 1) * n].reshape(-1) for k in range(LAYERS)]
        )
        at += LAYERS * n
    hidden = (
        dealt_tokens.astype(jnp.float32)
        + product(dealt_features, time_full)
        + time_shift.astype(jnp.float32)
    )
    full, kept_all = {}, []
    for layer in range(LAYERS):
        small = [v[layer] for v in vectors]
        raw, hidden = flow.step((raw, hidden))
        if layer == 0:
            gather_weights([("ffout", 1)], raw)
        raw, hidden = flow.until(lambda: boxes["qkv", layer][0], (raw, hidden))
        full["qkv", layer] = whole_weight("qkv", layer)
        full["out", layer] = whole_weight("out", layer)
        first, kept = attend(
            hidden, full["qkv", layer], full["out", layer], small, hide, heads
        )
        first, kept = flow.step((first, kept))
        first, kept = flow.until(lambda: boxes["ffin", layer][0], (first, kept))
        full["ffin", layer] = whole_weight("ffin", layer)
        active, slope = ffin_call(kept[-1], full["ffin", layer], small[4])
        first, active, slope = flow.step((first, active, slope))
        first, active, slope = flow.until(
            lambda: boxes["ffout", layer][0], (first, active, slope)
        )
        full["ffout", layer] = whole_weight("ffout", layer)
        hidden, resid_two = feed_out(first, active, full["ffout", layer], small)
        kept_all.append(kept + (slope, active, resid_two))

    final, ready = {}, {}
    orders = (up, down)

    def rep_stages(lanes):
        keeps = [keep for keep, _ in lanes]
        sends = [send for _, send in lanes]
        for at in range(len(up)):
            if at:
                cut = [split_columns(k, (me[0] // o[at]) % 2) for k, o in zip(keeps, orders)]
                keeps, sends = [k for k, _ in cut], [v for _, v in cut]
            keeps, got = yield (
                keeps,
                [swap_rep(v, o[at], n_rep) for v, o in zip(sends, orders)],
            )
            keeps = [add_low(k, v) for k, v in zip(keeps, got)]
        return keeps

    def reduce_stages(name, layer, left, right, partner):
        other_part = other_rows(me, left, right, n_shard)
        left, right, got = yield (left, right, swap_shard(other_part, 1, n_shard))
        lanes = own_rows(me, left, right, got, n_shard, [o[0] for o in orders])
        ready[name, layer] = yield from rep_stages(lanes)
        if (partner, layer) not in ready:
            return
        pieces, spans, at = [], {}, 0
        for key in ((partner, layer), (name, layer)):
            spans[key] = []
            for lane, piece in enumerate(ready[key]):
                n = piece.shape[2]
                for b in range(piece.shape[1] // R):
                    spans[key].append((b, lane, at, n))
                    pieces.append(piece[:, b * R : (b + 1) * R])
                    at += n
        shared = yield from finish_stages(jnp.concatenate(pieces, axis=2))
        for key, span in spans.items():
            final[key] = place_columns(shared, span, rep, orders)

    def finish_stages(pieces):
        for bit in bits_of(n_shard)[1:]:
            side = (me[1] // bit) % 2
            pair = pieces.reshape((pieces.shape[0] // 2, 2) + pieces.shape[1:])
            take = lambda at: lax.dynamic_index_in_dim(pair, at, axis=1, keepdims=False)
            keep, got = yield (take(side), swap_shard(take(1 - side), bit, n_shard))
            pieces = add_low(keep, got)
        have = pieces[0][None]
        for bit in bits_of(n_rep):
            have, got = yield (have, swap_rep(have, bit, n_rep))
            have = jnp.concatenate([have, got])
        return have

    def start(name, layer, left, right, partner):
        flow.add(reduce_stages(name, layer, left, right, partner))

    small_grads = {}
    hidden_b = hidden.astype(jnp.bfloat16)
    grad = dealt_cot.astype(jnp.float32)
    grad, hidden_b, kept_all[-1] = flow.step((grad, hidden_b, kept_all[-1]))
    for layer in reversed(range(LAYERS)):
        qv_b, out_b, gain_one, shift_one, ffin_b, ffout_b, gain_two, shift_two = [
            v[layer] for v in vectors
        ]
        hb, qkv_rows, logs, mixed, resid_one, first_b, slope, active, resid_two = kept_all[
            layer
        ]
        grad_two, grad_gain_two, grad_shift_two = norm_back(grad, resid_two, gain_two, shift_two)
        down_b = grad_two.astype(jnp.bfloat16)
        start("ffout", layer, active, down_b, "ffin")
        grad_inner = times_transposed(down_b, full["ffout", layer]) * slope.astype(jnp.float32)
        grad_inner = grad_inner.astype(jnp.bfloat16)
        grad_two, grad_inner = flow.step((grad_two, grad_inner))

        start("ffin", layer, first_b, grad_inner, "ffout")
        grad_first = grad_two + times_transposed(grad_inner, full["ffin", layer])
        grad_one, grad_gain_one, grad_shift_one = norm_back(
            grad_first, resid_one, gain_one, shift_one
        )
        attn_grad = grad_one.astype(jnp.bfloat16)
        grad_one, attn_grad = flow.step((grad_one, attn_grad))

        start("out", layer, mixed, attn_grad, "qkv")
        grad_qkv = attend_back(
            attn_grad, full["out", layer], qkv_rows, logs, hide, heads
        )
        if layer == LAYERS - 1:
            hidden_out = dot_rows(place_mat, hidden_b).astype(jnp.bfloat16)
            came_hidden = exchange(hidden_out)
        grad_one, grad_qkv, came_hidden = flow.step((grad_one, grad_qkv, came_hidden))

        start("qkv", layer, hb, grad_qkv, "out")
        grad = grad_one + times_transposed(grad_qkv, full["qkv", layer])
        small_grads[layer] = (
            jnp.concatenate(
                [column_sums(grad_qkv[:, :width]), column_sums(grad_qkv[:, 2 * width :])]
            ),
            column_sums(attn_grad),
            grad_gain_one,
            grad_shift_one,
            column_sums(grad_inner),
            column_sums(down_b),
            grad_gain_two,
            grad_shift_two,
        )
        grad, small_grads[layer] = flow.step((grad, small_grads[layer]))
    home_hidden = dot_rows(send_mat, came_hidden).astype(jnp.bfloat16)

    grad_embed = grad.astype(jnp.bfloat16)
    spread = [column_sums(grad_embed).reshape(n_shard, -1)]
    for k in range(len(small_args)):
        for layer in range(LAYERS):
            spread.append(small_grads[layer][k].reshape(n_shard, -1))
    spread = jnp.concatenate(spread, axis=1)
    used = spread.shape[1]
    spread = jnp.pad(spread, ((0, 0), (0, SMALL_ROWS * width - used)))
    n_z = n_shard // 2
    time_grad = contract_rows(dealt_features, grad_embed).reshape(n_z, 2, R, width)
    time_grad = jnp.concatenate(
        [time_grad, spread.reshape(n_z, 2, SMALL_ROWS, width)], axis=2
    ).astype(jnp.bfloat16)
    core = shard % 2
    pick = lambda at: lax.dynamic_index_in_dim(time_grad, at, axis=1, keepdims=False)

    def time_stages():
        keep, got = yield (pick(core), swap_shard(pick(1 - core), 1, n_shard))
        keep = add_low(keep, got)
        for bit in up:
            keep, send = split_columns(keep, (me[0] // bit) % 2)
            keep, got = yield (keep, swap_rep(send, bit, n_rep))
            keep = add_low(keep, got)
        shared = yield from finish_stages(keep)
        final["time"] = place_columns(shared, [(0, 0, 0, n_time)], rep, orders)

    flow.add(time_stages())
    came_grad = exchange(dot_rows(place_mat, grad_embed).astype(jnp.bfloat16))
    home_hidden, came_grad = flow.step((home_hidden, came_grad))
    home_grad = dot_rows(send_mat, came_grad).astype(jnp.bfloat16)
    while flow.live:
        home_grad = flow.step(home_grad)
    time_sum = final["time"]
    time_w_grad = time_sum[:R]
    small_sum = time_sum[R:].reshape(-1)
    at = time_bias.shape[0]
    time_b_grad = small_sum[:at]
    small_out = []
    for v in small_args:
        n = LAYERS * v.shape[1]
        small_out.append(small_sum[at : at + n].reshape(LAYERS, -1))
        at += n
    stack = {name: jnp.stack([final[name, k] for k in range(LAYERS)]) for name in arrays}
    return (
        home_hidden,
        home_grad,
        time_w_grad,
        time_b_grad,
        stack["qkv"],
        small_out[0],
        stack["out"],
        small_out[1],
        small_out[2],
        small_out[3],
        stack["ffin"],
        small_out[4],
        stack["ffout"],
        small_out[5],
        small_out[6],
        small_out[7],
    )


def solution(mesh):
    in_specs = (
        P(("rep", "shard"), None),
        P(("rep", "shard"), None),
        P(("rep", "shard"), None),
        P("rep"),
        P(("rep", "shard"), None),
        P(("rep", "shard"), None),
        P("shard", None),
        P("shard"),
        P(None, "shard", None),
        P(None, "shard"),
        P(None, "shard", None),
        P(None, "shard"),
        P(None, "shard"),
        P(None, "shard"),
        P(None, "shard", None),
        P(None, "shard"),
        P(None, "shard", None),
        P(None, "shard"),
        P(None, "shard"),
        P(None, "shard"),
    )
    out_specs = (
        P(("rep", "shard"), None),
        P(("rep", "shard"), None),
        P("shard", None),
        P("shard"),
        P(None, "shard", None),
        P(None, "shard"),
        P(None, "shard", None),
        P(None, "shard"),
        P(None, "shard"),
        P(None, "shard"),
        P(None, "shard", None),
        P(None, "shard"),
        P(None, "shard", None),
        P(None, "shard"),
        P(None, "shard"),
        P(None, "shard"),
    )
    body = functools.partial(
        per_device, n_rep=mesh.shape["rep"], n_shard=mesh.shape["shard"]
    )
    return jax.shard_map(
        body, mesh=mesh, in_specs=in_specs, out_specs=out_specs, check_vma=False
    )
```

```python
import functools
import math

import jax
import jax.numpy as jnp
from jax import lax
from jax.experimental import pallas as pl
from jax.experimental.pallas import tpu as pltpu
from jax.sharding import PartitionSpec as P

HEADS = 16
LAYERS = 2
SMALL_ROWS = 16


epsilon = 1e-05
negative = -1e30

def layer_norm(values, gain, shift):
    centred = values - jnp.mean(values, axis=-1, keepdims=True)
    spread = jnp.mean(centred * centred, axis=-1, keepdims=True)
    return centred * lax.rsqrt(spread + epsilon) * gain + shift


def product(left, right):
    return jnp.dot(left, right, preferred_element_type=jnp.float32)


def contract_rows(left, right):
    return lax.dot_general(
        left, right, (((0,), (0,)), ((), ())), preferred_element_type=jnp.float32
    )


def times_transposed(left, right):
    return lax.dot_general(
        left, right, (((1,), (1,)), ((), ())), preferred_element_type=jnp.float32
    )


def column_sums(values):
    return jnp.sum(values.astype(jnp.float32), axis=0)


def bits_of(count):
    return [1 << k for k in range(count.bit_length() - 1)]


def swap_rep(value, bit, n_rep):
    return lax.ppermute(value, "rep", [(i, i ^ bit) for i in range(n_rep)])


def swap_shard(value, bit, n_shard):
    return lax.ppermute(value, "shard", [(i, i ^ bit) for i in range(n_shard)])


def peers(count):
    return range(1, count)


def gather_chunk(pieces, n_rep, n_shard, box):
    piece = jnp.concatenate(pieces, axis=1) if len(pieces) > 1 else pieces[0]
    got = yield [swap_shard(piece, 2 * k, n_shard) for k in peers(n_shard // 2)]
    have = jnp.stack(got)
    have, core, sent = yield (
        have,
        swap_shard(have, 1, n_shard),
        [swap_rep(have, k, n_rep) for k in peers(n_rep)],
    )
    have, core, sent, other = yield (
        have,
        core,
        sent,
        [swap_shard(v, 1, n_shard) for v in sent],
    )
    box.extend([have] + sent + [core] + other)


class Flow:
    def __init__(self):
        self.live = []

    def add(self, stages):
        self.live.append((stages, next(stages)))

    def until(self, done, state):
        while not done():
            state = self.step(state)
        return state

    def step(self, state):
        values, state = lax.optimization_barrier(([v for _, v in self.live], state))
        before, self.live = self.live, []
        for (stages, _), value in zip(before, values):
            try:
                self.live.append((stages, stages.send(value)))
            except StopIteration:
                pass
        return state


def assemble_kernel(me_ref, local_ref, other_ref, *refs, spec):
    out_ref, buf, in_sem, out_sem = refs[-4:]
    layer, rows, cols, row_blocks, off, n = spec
    n_rep, n_z = (len(refs) - 4) // 2, refs[0].shape[0] + 1
    rep, shard = me_ref[0], me_ref[1]
    local, other = (v if layer is None else v.at[layer] for v in (local_ref, other_ref))
    height = rows * row_blocks
    per = cols // n

    def start(src, dst, at):
        pltpu.make_async_copy(src, dst, in_sem.at[at]).start()

    start(local, buf.at[pl.ds(shard * height, height), :], 0)
    start(other, buf.at[pl.ds((shard ^ 1) * height, height), :], 1)
    for flip in range(2, 2 * n_z):
        row0 = (shard ^ flip) * height
        for k in range(n_rep):
            p = rep ^ k
            block, col = (0, p) if row_blocks == 1 else (p // per, p % per)
            start(
                refs[(flip % 2) * n_rep + k].at[flip // 2 - 1, :, pl.ds(off, n)],
                buf.at[pl.ds(row0 + block * rows, rows), pl.ds(col * n, n)],
                flip,
            )
    for flip in range(2 * n_z):
        area = pl.ds((shard ^ flip) * height, height)
        pltpu.make_async_copy(buf.at[area, :], buf.at[area, :], in_sem.at[flip]).wait()
        pltpu.make_async_copy(buf.at[area, :], out_ref.at[area, :], out_sem).start()
    pltpu.make_async_copy(buf, out_ref, out_sem).wait()


def assemble(me, local, other, box, n_shard, spec):
    layer, rows, cols, row_blocks = spec[:4]
    any_spec = pl.BlockSpec(memory_space=pl.ANY)
    shape = (n_shard * rows * row_blocks, cols)
    return pl.pallas_call(
        functools.partial(assemble_kernel, spec=spec),
        out_shape=jax.ShapeDtypeStruct(shape, jnp.bfloat16),
        in_specs=[pl.BlockSpec(memory_space=pltpu.SMEM)] + [any_spec] * (2 + len(box)),
        out_specs=any_spec,
        scratch_shapes=[
            pltpu.VMEM(shape, jnp.bfloat16),
            pltpu.SemaphoreType.DMA((n_shard,)),
            pltpu.SemaphoreType.DMA,
        ],
    )(me, local, other, *box)


def ffin_kernel(x_ref, w_ref, b_ref, act_ref, slope_ref):
    inner = jnp.dot(x_ref[...], w_ref[...], preferred_element_type=jnp.float32)
    inner = inner + b_ref[...].astype(jnp.float32)
    phi_big = 0.5 * (1.0 + lax.erf(inner * math.sqrt(0.5)))
    density = jnp.exp(-0.5 * inner * inner) * (1.0 / math.sqrt(2.0 * math.pi))
    act_ref[...] = (inner * phi_big).astype(jnp.bfloat16)
    slope_ref[...] = (phi_big + inner * density).astype(jnp.bfloat16)


def ffin_call(x, w, b, tile=512):
    rows, width = x.shape
    wide = w.shape[1]
    out = jax.ShapeDtypeStruct((rows, wide), jnp.bfloat16)
    return pl.pallas_call(
        ffin_kernel,
        grid=(wide // tile,),
        out_shape=(out, out),
        in_specs=[
            pl.BlockSpec((rows, width), lambda i: (0, 0)),
            pl.BlockSpec((width, tile), lambda i: (0, i)),
            pl.BlockSpec((1, tile), lambda i: (0, i)),
        ],
        out_specs=(pl.BlockSpec((rows, tile), lambda i: (0, i)),) * 2,
    )(x, w, b.reshape(1, wide))


def dot_rows(left, right):
    return lax.dot_general(
        left, right, (((0,), (0,)), ((), ())), preferred_element_type=jnp.float32
    )


def other_kernel(me_ref, *refs):
    lefts, (right_ref, out_ref, turned) = refs[:-3], refs[-3:]
    height = out_ref.shape[1]

    @pl.when(pl.program_id(0) == 0)
    def _():
        for z, ref in enumerate(lefts):
            turned[z * height : (z + 1) * height, :] = ref[...].T

    total = product(turned[...], right_ref[...])
    out_ref[...] = total.reshape(out_ref.shape).astype(jnp.bfloat16)


def own_kernel(me_ref, *refs):
    lefts, (right_ref, came_ref), outs, turned = refs[:-7], refs[-7:-5], refs[-5:-1], refs[-1]
    height = came_ref.shape[1]
    step = pl.program_id(0)

    @pl.when(step == 0)
    def _():
        for z, ref in enumerate(lefts):
            turned[z * height : (z + 1) * height, :] = ref[...].T

    total = product(turned[...], right_ref[...]).reshape(came_ref.shape)
    total = (total + came_ref[...].astype(jnp.float32)).astype(jnp.bfloat16)
    for at, out_ref in enumerate(outs):

        @pl.when(step == at)
        def _():
            out_ref[...] = total


def other_rows(me, left, right, n_shard):
    tokens, depth = left.shape
    height, wide, n_z = depth // n_shard, right.shape[1], n_shard // 2
    if height % 128:
        full = contract_rows(left, right).astype(jnp.bfloat16)
        return jnp.stack(shard_pieces(full.reshape(n_shard, height, wide), me[1] ^ 1, n_z))
    tile = wide // 4
    return pl.pallas_call(
        other_kernel,
        grid_spec=pltpu.PrefetchScalarGridSpec(
            num_scalar_prefetch=1,
            grid=(4,),
            in_specs=[
                pl.BlockSpec((tokens, height), lambda i, m, z=z: (0, 2 * ((m[1] // 2) ^ z) + 1 - m[1] % 2))
                for z in range(n_z)
            ]
            + [pl.BlockSpec((tokens, tile), lambda i, m: (0, i))],
            out_specs=pl.BlockSpec((n_z, height, tile), lambda i, m: (0, 0, i)),
            scratch_shapes=[pltpu.VMEM((n_z * height, tokens), jnp.bfloat16)],
        ),
        out_shape=jax.ShapeDtypeStruct((n_z, height, wide), jnp.bfloat16),
    )(me, *([left] * n_z), right)


def own_rows(me, left, right, came, n_shard, bits):
    tokens, depth = left.shape
    height, wide, n_z = depth // n_shard, right.shape[1], n_shard // 2
    sides = [(me[0] // bit) % 2 for bit in bits]
    if height % 128:
        full = contract_rows(left, right).reshape(n_shard, height, wide)
        full = jnp.stack(shard_pieces(full, me[1], n_z))
        full = (full + came.astype(jnp.float32)).astype(jnp.bfloat16)
        halves = (full[:, :, : wide // 2], full[:, :, wide // 2 :])
        return [split_columns(v, side) for v, side in zip(halves, sides)]
    tile = wide // 4
    scalars = jnp.stack([sides[0], 1 - sides[0], 2 + sides[1], 3 - sides[1], me[1]])
    piece = jax.ShapeDtypeStruct((n_z, height, tile), jnp.bfloat16)
    outs = pl.pallas_call(
        own_kernel,
        grid_spec=pltpu.PrefetchScalarGridSpec(
            num_scalar_prefetch=1,
            grid=(4,),
            in_specs=[
                pl.BlockSpec(
                    (tokens, height),
                    lambda i, m, z=z: (0, 2 * ((m[4] // 2) ^ z) + m[4] % 2),
                )
                for z in range(n_z)
            ]
            + [
                pl.BlockSpec((tokens, tile), lambda i, m: (0, m[i])),
                pl.BlockSpec((n_z, height, tile), lambda i, m: (0, 0, m[i])),
            ],
            out_specs=(pl.BlockSpec((n_z, height, tile), lambda i, m: (0, 0, 0)),) * 4,
            scratch_shapes=[pltpu.VMEM((n_z * height, tokens), jnp.bfloat16)],
        ),
        out_shape=(piece,) * 4,
    )(scalars, *([left] * n_z), right, came)
    return [outs[:2], outs[2:]]


def split_columns(value, side):
    half = value.shape[-1] // 2
    take = lambda at: lax.dynamic_slice_in_dim(value, at * half, half, axis=value.ndim - 1)
    return take(side), take(1 - side)


def block_of(rep, order):
    block = 0
    for bit in order:
        block = block * 2 + (rep // bit) % 2
    return block


def shard_pieces(value, shard, n_z):
    return [lax.dynamic_index_in_dim(value, shard ^ (2 * k), keepdims=False) for k in range(n_z)]


def rep_columns(value, rep, n_rep):
    n = value.shape[-1] // n_rep
    at = value.ndim - 1
    return [lax.dynamic_slice_in_dim(value, (rep ^ k) * n, n, axis=at) for k in range(n_rep)]


def add_low(parts):
    return sum(v.astype(jnp.float32) for v in parts).astype(jnp.bfloat16)


def place_columns(shared, span, rep, orders):
    rows, n, n_rep = shared[0].shape[0], span[0][3], len(shared)
    blocks = 1 + max(b for b, _, _, _ in span)
    lanes = 1 + max(lane for _, lane, _, _ in span)
    whole = jnp.zeros((blocks * rows, lanes * n_rep * n), jnp.float32)
    for b, lane, off, _ in span:
        for k, value in enumerate(shared):
            part = value[:, off : off + n].astype(jnp.float32)
            to = lane * n_rep + block_of(rep ^ k, orders[lane])
            whole = lax.dynamic_update_slice(whole, part, (b * rows, to * n))
    return whole


def halve_kernel(m_ref, *refs, lanes):
    step = pl.program_id(0)
    for lane in range(lanes):
        total = add_low([refs[2 * lane][...], refs[2 * lane + 1][...]])
        for at in range(2):

            @pl.when(step == at)
            def _():
                refs[2 * lanes + 2 * lane + at][...] = total


def halve(keeps, gots, sides):
    n_z, height, wide = keeps[0].shape
    half, lanes = wide // 2, len(keeps)
    if half % 128:
        return [split_columns(add_low(v), s) for v, s in zip(zip(keeps, gots), sides)]
    scalars = jnp.stack([v for side in sides for v in (side, 1 - side)])
    block = lambda lane: pl.BlockSpec(
        (n_z, height, half), lambda i, m, lane=lane: (0, 0, m[2 * lane + i])
    )
    piece = jax.ShapeDtypeStruct((n_z, height, half), jnp.bfloat16)
    outs = pl.pallas_call(
        functools.partial(halve_kernel, lanes=lanes),
        grid_spec=pltpu.PrefetchScalarGridSpec(
            num_scalar_prefetch=1,
            grid=(2,),
            in_specs=[block(lane) for lane in range(lanes) for _ in range(2)],
            out_specs=(pl.BlockSpec((n_z, height, half), lambda i, m: (0, 0, 0)),)
            * (2 * lanes),
        ),
        out_shape=(piece,) * (2 * lanes),
    )(scalars, *[v for pair in zip(keeps, gots) for v in pair])
    return [outs[2 * lane : 2 * lane + 2] for lane in range(lanes)]


def merge_kernel(*refs, span, rows, n_z):
    ins, outs = refs[:-n_z], refs[-n_z:]
    for k in range(n_z):
        for b, source, at, n in span:
            area = slice(b * rows, (b + 1) * rows)
            outs[k][:, at : at + n] = add_low(
                [ins[2 * source][k, area, :], ins[2 * source + 1][k, area, :]]
            )


def merge(pairs, span, rows):
    n_z = pairs[0][0].shape[0]
    wide = sum(n for _, _, _, n in span)
    piece = jax.ShapeDtypeStruct((rows, wide), jnp.bfloat16)
    if any(n % 128 for _, _, _, n in span):
        sums = [add_low(v) for v in pairs]
        return [
            jnp.concatenate(
                [sums[j][k, b * rows : (b + 1) * rows] for b, j, _, _ in span], axis=1
            )
            for k in range(n_z)
        ]
    return list(
        pl.pallas_call(
            functools.partial(merge_kernel, span=tuple(span), rows=rows, n_z=n_z),
            out_shape=(piece,) * n_z,
        )(*[v for pair in pairs for v in pair])
    )


def place_kernel(to_ref, *refs, span, rows, count):
    ins, out_ref = refs[:count], refs[-1]
    for b, lane, off, n in span:
        for k in range(count):
            area = pl.ds(pl.multiple_of(to_ref[lane * count + k] * n, 128), n)
            out_ref[0, b * rows : (b + 1) * rows, area] = ins[k][:, off : off + n].astype(
                jnp.float32
            )


def place_layer(shared, span, rep, orders, layer, before):
    rows, count, n = shared[0].shape[0], len(shared), span[0][3]
    blocks = 1 + max(b for b, _, _, _ in span)
    shape = (LAYERS, blocks * rows, len(orders) * count * n)
    if n % 128:
        whole = place_columns(shared, span, rep, orders)[None]
        if before is None:
            before = jnp.zeros(shape, jnp.float32)
        return lax.dynamic_update_slice(before, whole, (layer, 0, 0))
    to = jnp.stack(
        [
            lane * count + block_of(rep ^ k, order)
            for lane, order in enumerate(orders)
            for k in range(count)
        ]
    )
    extra = [] if before is None else [before]
    return pl.pallas_call(
        functools.partial(place_kernel, span=tuple(span), rows=rows, count=count),
        grid=(1,),
        in_specs=[pl.BlockSpec(memory_space=pltpu.SMEM)]
        + [pl.BlockSpec(v.shape, lambda i: (0, 0)) for v in shared]
        + [pl.BlockSpec(memory_space=pl.ANY) for _ in extra],
        out_specs=pl.BlockSpec((1,) + shape[1:], lambda i: (layer, 0, 0)),
        out_shape=jax.ShapeDtypeStruct(shape, jnp.float32),
        input_output_aliases={1 + count: 0} if extra else {},
    )(to, *shared, *extra)


def inner_back_kernel(down_ref, w_ref, slope_ref, out_ref, sum_ref):
    grad = times_transposed(down_ref[...], w_ref[...]) * slope_ref[...].astype(jnp.float32)
    grad = grad.astype(jnp.bfloat16)
    out_ref[...] = grad
    sum_ref[...] = jnp.sum(grad.astype(jnp.float32), axis=0, keepdims=True)


def inner_back(down, w, slope, tile=512):
    rows, width = down.shape
    wide = slope.shape[1]
    grad, total = pl.pallas_call(
        inner_back_kernel,
        grid=(wide // tile,),
        in_specs=[
            pl.BlockSpec((rows, width), lambda i: (0, 0)),
            pl.BlockSpec((tile, width), lambda i: (i, 0)),
            pl.BlockSpec((rows, tile), lambda i: (0, i)),
        ],
        out_specs=(
            pl.BlockSpec((rows, tile), lambda i: (0, i)),
            pl.BlockSpec((1, tile), lambda i: (0, i)),
        ),
        out_shape=(
            jax.ShapeDtypeStruct((rows, wide), jnp.bfloat16),
            jax.ShapeDtypeStruct((1, wide), jnp.float32),
        ),
    )(down, w, slope)
    return grad, total[0]


def dot_low(left, right):
    return jnp.dot(left, right, preferred_element_type=jnp.float32).astype(jnp.bfloat16)


def low_lanes(shape, size):
    return lax.broadcasted_iota(jnp.int32, shape, 1) < size


def attend_kernel(q_ref, k_ref, v_ref, hide_ref, out_ref, log_ref, *, size):
    first = low_lanes(q_ref.shape, size)
    q, k, v, hide = q_ref[...], k_ref[...], v_ref[...], hide_ref[...]
    mixed, logs = [], []
    for h in range(2):
        mine = jnp.where(first if h == 0 else ~first, q, jnp.zeros_like(q))
        scores = times_transposed(mine, k) * (1.0 / math.sqrt(size)) + hide
        peak = jnp.max(scores, axis=-1, keepdims=True)
        expo = jnp.exp(scores - peak)
        total = jnp.sum(expo, axis=-1, keepdims=True)
        mixed.append(product((expo * (1.0 / total)).astype(jnp.bfloat16), v))
        logs.append(peak + jnp.log(total))
    out_ref[...] = jnp.where(first, mixed[0], mixed[1]).astype(jnp.bfloat16)
    log_ref[...] = jnp.where(first, logs[0], logs[1])


def attend_call(qkv_rows, hide, heads):
    rows, width = qkv_rows.shape[0], qkv_rows.shape[1] // 3
    pairs = heads // 2
    wide = width // pairs
    part = lambda k: pl.BlockSpec((rows, wide), lambda i, k=k: (0, k * pairs + i))
    return pl.pallas_call(
        functools.partial(attend_kernel, size=width // heads),
        grid=(pairs,),
        in_specs=[part(0), part(1), part(2), pl.BlockSpec((rows, rows), lambda i: (0, 0))],
        out_specs=(part(0), part(0)),
        out_shape=(
            jax.ShapeDtypeStruct((rows, width), jnp.bfloat16),
            jax.ShapeDtypeStruct((rows, width), jnp.float32),
        ),
    )(qkv_rows, qkv_rows, qkv_rows, hide)


def attend_back_kernel(
    q_ref, k_ref, v_ref, hide_ref, log_ref, grad_ref, w_ref, out_ref, *, size, width
):
    at = pl.program_id(0)
    first = low_lanes(q_ref.shape, size)
    q, k, v, hide = q_ref[...], k_ref[...], v_ref[...], hide_ref[...]
    scale = 1.0 / math.sqrt(size)
    grad = times_transposed(grad_ref[...], w_ref[...]).astype(jnp.bfloat16)
    parts = []
    for h in range(2):
        side = first if h == 0 else ~first
        mine = jnp.where(side, q, jnp.zeros_like(q))
        gone = jnp.where(side, grad, jnp.zeros_like(grad))
        scores = times_transposed(mine, k) * scale + hide
        probs = jnp.exp(scores - log_ref[:, h * size : h * size + 1])
        pull = times_transposed(gone, v)
        centre = jnp.sum(probs * pull, axis=-1, keepdims=True)
        back = (probs * (pull - centre)).astype(jnp.bfloat16)
        parts.append(
            (
                product(back, k) * scale,
                contract_rows(back, q) * scale,
                contract_rows(probs.astype(jnp.bfloat16), grad),
            )
        )
    for m in range(3):
        area = pl.ds(pl.multiple_of(m * width + at * 2 * size, 128), 2 * size)
        out_ref[:, area] = jnp.where(first, parts[0][m], parts[1][m]).astype(jnp.bfloat16)


def attend_back(attn_grad, out_w, qkv_rows, logs, hide, heads):
    rows, width = attn_grad.shape
    pairs = heads // 2
    wide = width // pairs
    part = lambda k: pl.BlockSpec((rows, wide), lambda i, k=k: (0, k * pairs + i))
    return pl.pallas_call(
        functools.partial(attend_back_kernel, size=width // heads, width=width),
        grid=(pairs,),
        in_specs=[
            part(0),
            part(1),
            part(2),
            pl.BlockSpec((rows, rows), lambda i: (0, 0)),
            part(0),
            pl.BlockSpec((rows, width), lambda i: (0, 0)),
            pl.BlockSpec((wide, width), lambda i: (i, 0)),
        ],
        out_specs=pl.BlockSpec((rows, 3 * width), lambda i: (0, 0)),
        out_shape=jax.ShapeDtypeStruct((rows, 3 * width), jnp.bfloat16),
    )(qkv_rows, qkv_rows, qkv_rows, hide, logs, attn_grad, out_w)


def attend(hidden, qkv_w, out_w, small, hide, heads):
    qv_b, out_b, gain_one, shift_one = small[:4]
    width = hidden.shape[1]
    hidden_b = hidden.astype(jnp.bfloat16)
    bias_full = jnp.concatenate(
        [qv_b[:width], jnp.zeros((width,), jnp.bfloat16), qv_b[width:]]
    ).astype(jnp.float32)
    qkv_rows = (product(hidden_b, qkv_w) + bias_full).astype(jnp.bfloat16)
    mixed, logs = attend_call(qkv_rows, hide, heads)
    resid_one = hidden + product(mixed, out_w) + out_b.astype(jnp.float32)
    first = layer_norm(resid_one, gain_one.astype(jnp.float32), shift_one.astype(jnp.float32))
    return first, (hidden_b, qkv_rows, logs, mixed, resid_one, first.astype(jnp.bfloat16))


def feed_out(first, active, ffout_w, small):
    ffout_b, gain_two, shift_two = small[5:]
    resid_two = first + product(active, ffout_w) + ffout_b.astype(jnp.float32)
    output = layer_norm(resid_two, gain_two.astype(jnp.float32), shift_two.astype(jnp.float32))
    return output, resid_two


def norm_back(grad, resid, gain, shift):
    _, pull = jax.vjp(layer_norm, resid, gain.astype(jnp.float32), shift.astype(jnp.float32))
    return pull(grad)


def per_device(
    tokens,
    time_features,
    out_grad,
    deal,
    seq_lengths,
    seq_offsets,
    time_weight,
    time_bias,
    qkv_weight,
    qv_bias,
    out_weight,
    out_bias,
    norm1_gain,
    norm1_bias,
    ffin_weight,
    ffin_bias,
    ffout_weight,
    ffout_bias,
    norm2_gain,
    norm2_bias,
    *,
    n_rep,
    n_shard,
):
    heads = HEADS
    rep, shard = lax.axis_index("rep"), lax.axis_index("shard")
    me = jnp.stack([rep, shard, jnp.zeros_like(rep), shard % 2]).astype(jnp.int32)
    rows, width = tokens.shape
    R = qkv_weight.shape[1]

    small_args = (
        qv_bias,
        out_bias,
        norm1_gain,
        norm1_bias,
        ffin_bias,
        ffout_bias,
        norm2_gain,
        norm2_bias,
    )
    flat = jnp.concatenate([time_bias] + [v.reshape(-1) for v in small_args])
    flat = jnp.pad(flat, (0, SMALL_ROWS * width - flat.shape[0])).reshape(SMALL_ROWS, width)
    time_ext = jnp.concatenate([time_weight, flat])

    mine = lax.dynamic_slice_in_dim(deal, shard * rows, rows)
    send_rank = jnp.sum((mine[None, :] < mine[:, None]).astype(jnp.int32), axis=1)
    slots = jnp.arange(rows, dtype=jnp.int32)
    send_mat = (send_rank[None, :] == slots[:, None]).astype(jnp.bfloat16)
    given = jnp.arange(deal.shape[0], dtype=jnp.int32)
    hit = deal[:, None] == (shard * rows + slots)[None, :]
    source = jnp.sum(jnp.where(hit, (given // rows)[:, None], 0), axis=0)
    key = source * rows + slots
    place = jnp.sum((key[None, :] < key[:, None]).astype(jnp.int32), axis=1)
    place_mat = (place[:, None] == slots[None, :]).astype(jnp.bfloat16)

    def exchange(value):
        return lax.all_to_all(value, "shard", split_axis=0, concat_axis=0, tiled=True)

    starts = seq_offsets[0][:, None]
    finish = starts + seq_lengths[0][:, None]
    member = (slots[None, :] >= starts) & (slots[None, :] < finish)
    visible = jnp.any(member[:, :, None] & member[:, None, :], axis=0) | (
        slots[:, None] == slots[None, :]
    )
    hide = jnp.where(visible, 0.0, negative).astype(jnp.float32)

    names = ("qkv", "out", "ffin", "ffout")
    arrays = {
        "qkv": (qkv_weight, 1),
        "out": (out_weight, 1),
        "ffin": (ffin_weight, 1),
        "ffout": (ffout_weight, ffout_weight.shape[1] // R),
    }
    time_rows = R + SMALL_ROWS
    me2 = jnp.stack([rep, shard]).astype(jnp.int32)
    other = {name: swap_shard(arrays[name][0], 1, n_shard) for name in names}

    def rep_slice(array, layer, blocks):
        if blocks == 1:
            n = array.shape[2] // n_rep
            return lax.dynamic_slice(array, (layer, 0, rep * n), (1, R, n))[0]
        per = n_rep // blocks
        n = array.shape[2] // per
        return lax.dynamic_slice(
            array, (layer, (rep // per) * R, (rep % per) * n), (1, R, n)
        )[0]

    flow = Flow()
    boxes = {}

    def gather_weights(members, raw):
        pieces = [rep_slice(raw[name], layer, arrays[name][1]) for name, layer in members]
        box, at = [], 0
        for (name, layer), piece in zip(members, pieces):
            boxes[name, layer] = (box, at, piece.shape[1])
            at += piece.shape[1]
        flow.add(gather_chunk(pieces, n_rep, n_shard, box))

    def whole_weight(name, layer):
        array, blocks = arrays[name]
        box, off, n = boxes[name, layer]
        spec = (layer, R, array.shape[2], blocks, off, n)
        return assemble(me2, array, other[name], box, n_shard, spec)

    raw = {name: arrays[name][0] for name in names}
    n_time = width // n_rep
    time_box = []
    time_piece = lax.dynamic_slice_in_dim(time_ext, rep * n_time, n_time, axis=1)
    flow.add(gather_chunk([time_piece], n_rep, n_shard, time_box))
    time_other = swap_shard(time_ext, 1, n_shard)
    gather_weights([("qkv", 0), ("out", 0)], raw)
    rows_out = dot_low(send_mat, jnp.concatenate([tokens, time_features], axis=1))
    raw, rows_out, cot = flow.step((raw, rows_out, out_grad))
    gather_weights([("ffin", 0)], raw)
    came = exchange(rows_out)
    raw, came, cot = flow.step((raw, came, cot))
    gather_weights([("ffout", 0)], raw)
    dealt = dot_low(place_mat, came)
    dealt_tokens, dealt_features = dealt[:, :width], dealt[:, width:]
    raw, dealt_tokens, dealt_features, cot, time_other = flow.step(
        (raw, dealt_tokens, dealt_features, cot, time_other)
    )
    gather_weights([("qkv", 1), ("out", 1)], raw)
    raw = flow.until(lambda: time_box, raw)

    spec = (None, time_rows, width, 1, 0, n_time)
    time_all = assemble(me2, time_ext, time_other, time_box, n_shard, spec)
    time_all = time_all.reshape(n_shard, time_rows, width)
    time_full = time_all[:, :R].reshape(n_shard * R, width)
    small_all = time_all[:, R:].reshape(n_shard, SMALL_ROWS * width)
    at = time_bias.shape[0]
    time_shift = small_all[:, :at].reshape(-1)
    vectors = []
    for v in small_args:
        n = v.shape[1]
        vectors.append(
            [small_all[:, at + k * n : at + (k + 1) * n].reshape(-1) for k in range(LAYERS)]
        )
        at += LAYERS * n
    hidden = (
        dealt_tokens.astype(jnp.float32)
        + product(dealt_features, time_full)
        + time_shift.astype(jnp.float32)
    )
    full, kept_all = {}, []
    for layer in range(LAYERS):
        small = [v[layer] for v in vectors]
        if layer:
            hidden = flow.step(hidden)
        raw, hidden = flow.until(lambda: boxes["qkv", layer][0], (raw, hidden))
        full["qkv", layer] = whole_weight("qkv", layer)
        full["out", layer] = whole_weight("out", layer)
        first, kept = attend(
            hidden, full["qkv", layer], full["out", layer], small, hide, heads
        )
        raw, first, kept, cot = flow.step((raw, first, kept, cot))
        if layer == 0:
            gather_weights([("ffin", 1)], raw)
            cot = exchange(dot_low(send_mat, cot))
        first, kept = flow.until(lambda: boxes["ffin", layer][0], (first, kept))
        full["ffin", layer] = whole_weight("ffin", layer)
        active, slope = ffin_call(kept[-1], full["ffin", layer], small[4])
        raw, first, active, slope, cot = flow.step((raw, first, active, slope, cot))
        if layer == 0:
            gather_weights([("ffout", 1)], raw)
        first, active, slope = flow.until(
            lambda: boxes["ffout", layer][0], (first, active, slope)
        )
        full["ffout", layer] = whole_weight("ffout", layer)
        hidden, resid_two = feed_out(first, active, full["ffout", layer], small)
        kept_all.append(kept + (slope, active, resid_two))

    final, ready = {}, {}

    def rep_stage(parts):
        keep, got = yield (parts[0], [swap_rep(parts[k], k, n_rep) for k in peers(n_rep)])
        return add_low([keep] + got)

    def finish_stages(pieces):
        keep, got = yield (
            pieces[0],
            [swap_shard(pieces[k], 2 * k, n_shard) for k in peers(n_shard // 2)],
        )
        total = add_low([keep] + got)
        total, got = yield (total, [swap_rep(total, k, n_rep) for k in peers(n_rep)])
        return [total] + got

    bits = bits_of(n_rep)
    orders = (bits, bits[::-1])

    def lane_stages(lanes):
        keeps, sends = [v for v, _ in lanes], [v for _, v in lanes]
        for at in range(len(bits)):
            if at:
                cut = halve(keeps, got, [(rep // o[at]) % 2 for o in orders])
                keeps, sends = [k for k, _ in cut], [v for _, v in cut]
            keeps, got = yield (
                keeps,
                [swap_rep(v, o[at], n_rep) for v, o in zip(sends, orders)],
            )
        return list(zip(keeps, got))

    def reduce_stages(name, layer, left, right, partner):
        got = swap_shard(other_rows(me, left, right, n_shard), 1, n_shard)
        lanes = yield own_rows(me, left, right, got, n_shard, [o[0] for o in orders])
        ready[name, layer] = yield from lane_stages(lanes)
        if (partner, layer) not in ready:
            return
        pairs, whole, spans, at = [], [], {}, 0
        for key in ((partner, layer), (name, layer)):
            spans[key] = []
            for lane, pair in enumerate(ready[key]):
                n = pair[0].shape[2]
                for b in range(pair[0].shape[1] // R):
                    spans[key].append((b, lane, at, n))
                    whole.append((b, len(pairs), at, n))
                    at += n
                pairs.append(pair)
        shared = yield from finish_stages(merge(pairs, whole, R))
        for key, span in spans.items():
            final[key[0]] = place_layer(
                shared, span, rep, orders, layer, final.get(key[0])
            )

    def start(name, layer, left, right, partner):
        flow.add(reduce_stages(name, layer, left, right, partner))

    small_grads = {}
    hidden_b = hidden.astype(jnp.bfloat16)
    grad = dot_low(place_mat, cot).astype(jnp.float32)
    grad, hidden_b, kept_all[-1] = flow.step((grad, hidden_b, kept_all[-1]))
    for layer in reversed(range(LAYERS)):
        qv_b, out_b, gain_one, shift_one, ffin_b, ffout_b, gain_two, shift_two = [
            v[layer] for v in vectors
        ]
        hb, qkv_rows, logs, mixed, resid_one, first_b, slope, active, resid_two = kept_all[
            layer
        ]
        grad_two, grad_gain_two, grad_shift_two = norm_back(grad, resid_two, gain_two, shift_two)
        down_b = grad_two.astype(jnp.bfloat16)
        start("ffout", layer, active, down_b, "ffin")
        grad_inner, grad_ffin_bias = inner_back(down_b, full["ffout", layer], slope)
        grad_two, grad_inner = flow.step((grad_two, grad_inner))

        start("ffin", layer, first_b, grad_inner, "ffout")
        grad_first = grad_two + times_transposed(grad_inner, full["ffin", layer])
        grad_one, grad_gain_one, grad_shift_one = norm_back(
            grad_first, resid_one, gain_one, shift_one
        )
        attn_grad = grad_one.astype(jnp.bfloat16)
        grad_one, attn_grad = flow.step((grad_one, attn_grad))

        start("out", layer, mixed, attn_grad, "qkv")
        grad_qkv = attend_back(
            attn_grad, full["out", layer], qkv_rows, logs, hide, heads
        )
        if layer == LAYERS - 1:
            hidden_out = dot_rows(place_mat, hidden_b).astype(jnp.bfloat16)
            came_hidden = exchange(hidden_out)
        grad_one, grad_qkv, came_hidden = flow.step((grad_one, grad_qkv, came_hidden))

        start("qkv", layer, hb, grad_qkv, "out")
        grad = grad_one + times_transposed(grad_qkv, full["qkv", layer])
        small_grads[layer] = (
            jnp.concatenate(
                [column_sums(grad_qkv[:, :width]), column_sums(grad_qkv[:, 2 * width :])]
            ),
            column_sums(attn_grad),
            grad_gain_one,
            grad_shift_one,
            grad_ffin_bias,
            column_sums(down_b),
            grad_gain_two,
            grad_shift_two,
        )
        grad, small_grads[layer] = flow.step((grad, small_grads[layer]))
    home_hidden = dot_rows(send_mat, came_hidden).astype(jnp.bfloat16)

    grad_embed = grad.astype(jnp.bfloat16)
    spread = [column_sums(grad_embed).reshape(n_shard, -1)]
    for k in range(len(small_args)):
        for layer in range(LAYERS):
            spread.append(small_grads[layer][k].reshape(n_shard, -1))
    spread = jnp.concatenate(spread, axis=1)
    used = spread.shape[1]
    spread = jnp.pad(spread, ((0, 0), (0, SMALL_ROWS * width - used)))
    n_z = n_shard // 2
    time_grad = contract_rows(dealt_features, grad_embed).reshape(n_shard, R, width)
    time_grad = jnp.concatenate(
        [time_grad, spread.reshape(n_shard, SMALL_ROWS, width)], axis=1
    ).astype(jnp.bfloat16)
    pick = lambda at: jnp.stack(shard_pieces(time_grad, at, n_z))

    def time_stages():
        keep, got = yield (pick(shard), swap_shard(pick(shard ^ 1), 1, n_shard))
        total = yield from rep_stage(rep_columns(add_low([keep, got]), rep, n_rep))
        shared = yield from finish_stages([total[k] for k in range(n_z)])
        final["time"] = place_columns(shared, [(0, 0, 0, n_time)], rep, [bits[::-1]])

    flow.add(time_stages())
    came_grad = exchange(dot_rows(place_mat, grad_embed).astype(jnp.bfloat16))
    while flow.live:
        home_hidden = flow.step(home_hidden)
    home_grad = dot_rows(send_mat, came_grad).astype(jnp.bfloat16)
    time_sum = final["time"]
    time_w_grad = time_sum[:R]
    small_sum = time_sum[R:].reshape(-1)
    at = time_bias.shape[0]
    time_b_grad = small_sum[:at]
    small_out = []
    for v in small_args:
        n = LAYERS * v.shape[1]
        small_out.append(small_sum[at : at + n].reshape(LAYERS, -1))
        at += n
    return (
        home_hidden,
        home_grad,
        time_w_grad,
        time_b_grad,
        final["qkv"],
        small_out[0],
        final["out"],
        small_out[1],
        small_out[2],
        small_out[3],
        final["ffin"],
        small_out[4],
        final["ffout"],
        small_out[5],
        small_out[6],
        small_out[7],
    )


def solution(mesh):
    in_specs = (
        P(("rep", "shard"), None),
        P(("rep", "shard"), None),
        P(("rep", "shard"), None),
        P("rep"),
        P(("rep", "shard"), None),
        P(("rep", "shard"), None),
        P("shard", None),
        P("shard"),
        P(None, "shard", None),
        P(None, "shard"),
        P(None, "shard", None),
        P(None, "shard"),
        P(None, "shard"),
        P(None, "shard"),
        P(None, "shard", None),
        P(None, "shard"),
        P(None, "shard", None),
        P(None, "shard"),
        P(None, "shard"),
        P(None, "shard"),
    )
    out_specs = (
        P(("rep", "shard"), None),
        P(("rep", "shard"), None),
        P("shard", None),
        P("shard"),
        P(None, "shard", None),
        P(None, "shard"),
        P(None, "shard", None),
        P(None, "shard"),
        P(None, "shard"),
        P(None, "shard"),
        P(None, "shard", None),
        P(None, "shard"),
        P(None, "shard", None),
        P(None, "shard"),
        P(None, "shard"),
        P(None, "shard"),
    )
    body = functools.partial(
        per_device, n_rep=mesh.shape["rep"], n_shard=mesh.shape["shard"]
    )
    return jax.shard_map(
        body, mesh=mesh, in_specs=in_specs, out_specs=out_specs, check_vma=False
    )
```
